32 devices in a mesh: grp: 2 (over x), row: 16 (over z, y, core).
Axes of the slice: x: 2, y: 2, z: 4, core: 2. Of those that a mesh axis runs over, the one named last changes fastest.
Arguments:
- system: float32 [32768, 16384], P(('grp', 'row')), parts along dimension 0, may hold values from -150 to 150
- measured: float32 [32768, 512], P(('grp', 'row')), parts along dimension 0, may hold values from -24 to 24
- row_class: int32 [32768], P(('grp', 'row')), parts along dimension 0, may hold values from 0 to 7
- band_weight: float32 [16], P('grp'), parts along dimension 0, may hold values from 0.3 to 1.5
- order: int32 [32, 2], P(('grp', 'row')), parts along dimension 0, may hold values from 0 to 1, each once within a row
Outputs:
- reconstruction: float32 [1024, 16384], P(('grp', 'row')), parts along dimension 0
The draws below stay inside these ranges and needn't reach their ends.
There are 2 independent parts, one for each index of `grp`. The reference program is written for one: setup_inputs(seed, part) draws one part's arguments, and reference() takes and returns one part's arrays. A program takes and returns all parts, laid end to end along the dimension named above; each array names one. Nothing has to cross between parts.
All inputs are finite; a program needn't handle non-finite values.
Results may differ from the reference program's by a relative error of at most 0.0001.
Values sent between devices are 32-bit elements; how exact they have to be, the bound alone decides.
No kernel may reach another device: no remote copies, remote signals or barrier semaphores. Data moves between devices by JAX's collectives and lax.ppermute only.
A program may use at most 128 MiB of HBM per device.

```python
import math
import jax
import jax.numpy as jnp
from jax import lax

M = 16384
V = 16384
BATCH_FRAMES = 32
STEPS = 6
SUBBLOCK_COUNT = 2
BANDS = 8
NBLK = 16
FRAMES = 512
N_ROW = 16


def draw_system(key, part):
    key_base, key_rows, key_cols = jax.random.split(key, 3)
    base = jnp.clip(jax.random.normal(key_base, (M, V), jnp.float32), -6.0, 6.0)
    lower = math.log(0.5)
    upper = math.log(5.0)
    row_scale = jnp.exp(jax.random.uniform(key_rows, (M, 1), jnp.float32, lower, upper))
    col_scale = jnp.exp(jax.random.uniform(key_cols, (1, V), jnp.float32, lower, upper))
    return base * row_scale * col_scale


def plant(result, own_key, least, top_value):
    index_at = [jax.random.randint(jax.random.fold_in(own_key, axis), (), 0, length) for axis, length in enumerate(result.shape)]
    main_axis = result.shape.index(max(result.shape))
    neighbour = index_at[:main_axis] + [(index_at[main_axis] + 1) % result.shape[main_axis]] + index_at[main_axis + 1:]
    return result.at[tuple(index_at)].set(least).at[tuple(neighbour)].set(top_value)


def shard_levels(rng, shape, shards, least, largest):
    def one(axis_at, shards_of):
        steps = jax.random.uniform(jax.random.fold_in(jax.random.fold_in(rng, 6), axis_at), (shards_of,), jnp.float32, least / len(shards), largest / len(shards))
        return jnp.repeat(jnp.exp(steps), shape[axis_at] // shards_of).reshape((-1,) + (1,) * (len(shape) - axis_at - 1))

    loudness = one(*shards[0])
    for cut in shards[1:]:
        loudness = loudness * one(*cut)
    return loudness


def scatter_about(stream_key, shape, width, reach, cuts=(), kind=jnp.bfloat16):
    result = width * jax.random.normal(stream_key, shape, jnp.float32)
    if cuts:
        result = result * shard_levels(stream_key, shape, cuts, -0.22, 0.18)
    return jnp.clip(result, -reach, reach).astype(kind)


def setup_inputs(seed: int = 0, part: int = 0) -> dict:
    key_list = jax.random.split(jax.random.key(seed), 6)
    part_keys = jax.random.split(jax.random.fold_in(key_list[5], part), 6)
    return {
        "system": draw_system(jax.random.fold_in(jax.random.fold_in(key_list[5], part), 71), part),
        "measured": scatter_about(part_keys[1], (M, FRAMES), 4.0, 24.0, ((0, 16),), jnp.float32),
        "row_class": plant(jax.random.randint(part_keys[2], (M,), 0, BANDS), jax.random.fold_in(part_keys[2], 1), 0, BANDS - 1).astype(jnp.int32),
        "band_weight": jnp.clip(jnp.exp(jax.random.uniform(part_keys[3], (BANDS,), jnp.float32, math.log(0.3), math.log(1.5))), 0.3, 1.5),
        "order": jax.vmap(lambda own: jax.random.permutation(own, SUBBLOCK_COUNT))(jax.random.split(part_keys[4], NBLK)).reshape((NBLK, SUBBLOCK_COUNT)).astype(jnp.int32),
    }


epsilon = 1e-6


def reference(system, measured, row_class, band_weight, order):
    total_blocks = N_ROW
    block_rows = M // total_blocks
    subblock_rows = block_rows // SUBBLOCK_COUNT
    band_hits = (row_class[:, None] == jnp.arange(BANDS, dtype=jnp.int32)[None, :]).astype(jnp.float32)
    row_weight = jnp.dot(band_hits, band_weight, precision=lax.Precision.HIGHEST) / (jnp.sum(system * system, axis=1) + epsilon)
    block_matrix = system.reshape(total_blocks, SUBBLOCK_COUNT, subblock_rows, V)
    block_weight = row_weight.reshape(total_blocks, SUBBLOCK_COUNT, subblock_rows)
    block_signal = measured.reshape(total_blocks, SUBBLOCK_COUNT, subblock_rows, total_blocks, BATCH_FRAMES)
    pictures = jnp.zeros((total_blocks, BATCH_FRAMES, V), jnp.float32)
    block_numbers = jnp.arange(total_blocks, dtype=jnp.int32)

    def visit(packed_values):
        local_matrix, local_weight, local_signal, local_ordering, particle_image = packed_values
        for which in range(SUBBLOCK_COUNT):
            selected_block = local_ordering[which]
            sub_matrix = local_matrix[selected_block]
            sub_weight = local_weight[selected_block]
            observed_signal = local_signal[selected_block]
            forward = jnp.einsum('fv,rv->fr', particle_image, sub_matrix, precision=lax.Precision.HIGHEST)
            residual = observed_signal.T - forward
            particle_image = jnp.maximum(particle_image + jnp.einsum('fr,rv->fv', residual * sub_weight[None, :], sub_matrix, precision=lax.Precision.HIGHEST), 0.0)
        return particle_image

    for visit_no in range(STEPS):
        block_holders = (block_numbers - visit_no) % total_blocks
        carried = pictures[block_holders]
        observed_full = block_signal[block_numbers, :, :, block_holders, :]
        carried = lax.map(visit, (block_matrix, block_weight, observed_full, order, carried))
        pictures = pictures.at[block_holders].set(carried)
    return pictures.reshape(total_blocks * BATCH_FRAMES, V)
```

```python
import jax
import jax.numpy as jnp
from jax import lax
from jax.sharding import PartitionSpec as P

BATCH_FRAMES = 32
STEPS = 6


epsilon = 1e-06


def shifted(value, axis, steps):
    count = lax.axis_size(axis)
    pairs = [(source, (source + steps) % count) for source in range(count)]
    return lax.ppermute(value, axis, pairs)


def local(system, measured, row_class, band_weight, order):
    cycle_size = lax.axis_size("row")
    position = lax.axis_index("row")
    rows_here = system.shape[0]
    voxels = system.shape[1]
    subblocks = order.shape[1]
    subblock_rows = rows_here // subblocks
    band_hits = (
        row_class[:, None] == jnp.arange(band_weight.shape[0], dtype=jnp.int32)[None, :]
    ).astype(jnp.float32)
    row_weight = jnp.dot(band_hits, band_weight, precision=lax.Precision.HIGHEST) / (
        jnp.sum(system * system, axis=1) + epsilon
    )
    sequence = order[0]
    ordered = []
    for which in range(subblocks):
        first_row = sequence[which] * subblock_rows
        ordered.append(
            (
                lax.dynamic_slice_in_dim(system, first_row, subblock_rows, 0),
                lax.dynamic_slice_in_dim(row_weight, first_row, subblock_rows, 0),
                first_row,
            )
        )
    particle_image = jnp.zeros((BATCH_FRAMES, voxels), jnp.float32)
    for visit_no in range(STEPS):
        visit_particle_image = particle_image
        frame_count = visit_particle_image.shape[0]
        owner = (position - visit_no) % cycle_size
        first_frame = owner * BATCH_FRAMES
        for visit_which, (sub_matrix, sub_weight, visit_first_row) in enumerate(ordered):
            observed_signal = lax.dynamic_slice(
                measured, (visit_first_row, first_frame), (subblock_rows, frame_count)
            )
            if visit_no == 0 and visit_which == 0:
                residual = observed_signal.T
            else:
                forward = jnp.einsum(
                    "fv,rv->fr", visit_particle_image, sub_matrix, precision=lax.Precision.HIGH
                )
                residual = observed_signal.T - forward
            visit_particle_image = jnp.maximum(
                visit_particle_image
                + jnp.einsum(
                    "fr,rv->fv",
                    residual * sub_weight[None, :],
                    sub_matrix,
                    precision=lax.Precision.HIGH,
                ),
                0.0,
            )
        particle_image = visit_particle_image
        if visit_no + 1 < STEPS:
            particle_image = shifted(particle_image, "row", 1)
    return shifted(particle_image, "row", 1 - STEPS)


def solution(mesh):
    return jax.shard_map(
        local,
        mesh=mesh,
        in_specs=(
            P(("grp", "row"), None),
            P(("grp", "row"), None),
            P(("grp", "row")),
            P("grp"),
            P(("grp", "row"), None),
        ),
        out_specs=P(("grp", "row"), None),
        check_vma=False,
    )
```

```python
import jax
import jax.numpy as jnp
from jax import lax
from jax.sharding import PartitionSpec as P

BATCH_FRAMES = 32
STEPS = 6
CHUNKS = 4


epsilon = 1e-06


def shifted(value, axis, steps):
    count = lax.axis_size(axis)
    pairs = [(source, (source + steps) % count) for source in range(count)]
    return lax.ppermute(value, axis, pairs)


def forward_of(chunks, sub_matrix, width):
    total = None
    for index, chunk in enumerate(chunks):
        part = jnp.einsum(
            "fv,rv->fr",
            chunk,
            sub_matrix[:, index * width:(index + 1) * width],
            precision=lax.Precision.HIGH,
        )
        total = part if total is None else total + part
    return total


def updated(chunks, weighted, sub_matrix, width):
    return [
        jnp.maximum(
            chunk
            + jnp.einsum(
                "fr,rv->fv",
                weighted,
                sub_matrix[:, index * width:(index + 1) * width],
                precision=lax.Precision.HIGH,
            ),
            0.0,
        )
        for index, chunk in enumerate(chunks)
    ]


def local(system, measured, row_class, band_weight, order):
    cycle_size = lax.axis_size("row")
    position = lax.axis_index("row")
    rows_here = system.shape[0]
    voxels = system.shape[1]
    subblocks = order.shape[1]
    subblock_rows = rows_here // subblocks
    width = voxels // CHUNKS
    band_hits = (
        row_class[:, None] == jnp.arange(band_weight.shape[0], dtype=jnp.int32)[None, :]
    ).astype(jnp.float32)
    row_weight = jnp.dot(band_hits, band_weight, precision=lax.Precision.HIGHEST) / (
        jnp.sum(system * system, axis=1) + epsilon
    )
    sequence = order[0]
    ordered = []
    for which in range(subblocks):
        first_row = sequence[which] * subblock_rows
        ordered.append(
            (
                lax.dynamic_slice_in_dim(system, first_row, subblock_rows, 0),
                lax.dynamic_slice_in_dim(row_weight, first_row, subblock_rows, 0),
                first_row,
            )
        )
    chunks = [jnp.zeros((BATCH_FRAMES, width), jnp.float32) for _ in range(CHUNKS)]
    for visit_no in range(STEPS):
        owner = (position - visit_no) % cycle_size
        first_frame = owner * BATCH_FRAMES
        for visit_which, (sub_matrix, sub_weight, visit_first_row) in enumerate(ordered):
            observed_signal = lax.dynamic_slice(
                measured, (visit_first_row, first_frame), (subblock_rows, BATCH_FRAMES)
            )
            if visit_no == 0 and visit_which == 0:
                residual = observed_signal.T
            else:
                residual = observed_signal.T - forward_of(chunks, sub_matrix, width)
            chunks = updated(chunks, residual * sub_weight[None, :], sub_matrix, width)
        steps = 1 if visit_no + 1 < STEPS else 1 - STEPS
        chunks = [shifted(chunk, "row", steps) for chunk in chunks]
    return jnp.concatenate(chunks, axis=1)


def solution(mesh):
    return jax.shard_map(
        local,
        mesh=mesh,
        in_specs=(
            P(("grp", "row"), None),
            P(("grp", "row"), None),
            P(("grp", "row")),
            P("grp"),
            P(("grp", "row"), None),
        ),
        out_specs=P(("grp", "row"), None),
        check_vma=False,
    )
```

```python
import jax
import jax.numpy as jnp
from jax import lax
from jax.experimental import pallas as pl
from jax.experimental.pallas import tpu as pltpu
from jax.sharding import PartitionSpec as P

BATCH_FRAMES = 32
STEPS = 6


epsilon = 1e-06


def shifted(value, axis, steps):
    count = lax.axis_size(axis)
    pairs = [(source, (source + steps) % count) for source in range(count)]
    return lax.ppermute(value, axis, pairs)


TILE = 2048
_DN = (((1,), (1,)), ((), ()))


def _split(value):
    high = value.astype(jnp.bfloat16)
    return high, (value - high.astype(jnp.float32)).astype(jnp.bfloat16)


def _forward_kernel(offset_ref, image_ref, matrix_ref, out_ref):
    @pl.when(pl.program_id(0) == 0)
    def _():
        out_ref[...] = jnp.zeros_like(out_ref)

    frames = image_ref.shape[0]
    image_hi, image_lo = _split(image_ref[...])
    both = jnp.concatenate([image_hi, image_lo], axis=0)
    matrix_hi, matrix_lo = _split(matrix_ref[...])
    paired = lax.dot_general(matrix_hi, both, _DN, preferred_element_type=jnp.float32)
    cross = lax.dot_general(matrix_lo, image_hi, _DN, preferred_element_type=jnp.float32)
    out_ref[...] += paired[:, :frames] + paired[:, frames:] + cross


def forward_t(image, system, block, rows):
    frames, voxels = image.shape
    tile = min(TILE, voxels)
    return pl.pallas_call(
        _forward_kernel,
        out_shape=jax.ShapeDtypeStruct((rows, frames), jnp.float32),
        grid_spec=pltpu.PrefetchScalarGridSpec(
            num_scalar_prefetch=1,
            grid=(voxels // tile,),
            in_specs=[
                pl.BlockSpec((frames, tile), lambda j, off: (0, j)),
                pl.BlockSpec((rows, tile), lambda j, off: (off[0], j)),
            ],
            out_specs=pl.BlockSpec((rows, frames), lambda j, off: (0, 0)),
        ),
        compiler_params=pltpu.CompilerParams(
            dimension_semantics=("arbitrary",), vmem_limit_bytes=48 * 1024 * 1024
        ),
        cost_estimate=pl.CostEstimate(
            flops=2 * rows * voxels * frames * 3,
            transcendentals=0,
            bytes_accessed=4 * (rows * voxels + frames * voxels + rows * frames),
        ),
    )(block, image, system)


def _update_kernel(offset_ref, weighted_ref, image_ref, matrix_ref, out_ref):
    frames = image_ref.shape[0]
    weighted_hi, weighted_lo = _split(weighted_ref[...])
    both = jnp.concatenate([weighted_hi, weighted_lo], axis=0)
    matrix_hi, matrix_lo = _split(matrix_ref[...])
    paired = jnp.dot(both, matrix_hi, preferred_element_type=jnp.float32)
    cross = jnp.dot(weighted_hi, matrix_lo, preferred_element_type=jnp.float32)
    out_ref[...] = jnp.maximum(
        image_ref[...] + (paired[:frames] + paired[frames:] + cross), 0.0
    )


def update(weighted, image, system, block, rows):
    frames, voxels = image.shape
    tile = min(TILE, voxels)
    return pl.pallas_call(
        _update_kernel,
        out_shape=jax.ShapeDtypeStruct((frames, voxels), jnp.float32),
        grid_spec=pltpu.PrefetchScalarGridSpec(
            num_scalar_prefetch=1,
            grid=(voxels // tile,),
            in_specs=[
                pl.BlockSpec((frames, rows), lambda j, off: (0, 0)),
                pl.BlockSpec((frames, tile), lambda j, off: (0, j)),
                pl.BlockSpec((rows, tile), lambda j, off: (off[0], j)),
            ],
            out_specs=pl.BlockSpec((frames, tile), lambda j, off: (0, j)),
        ),
        compiler_params=pltpu.CompilerParams(
            dimension_semantics=("arbitrary",), vmem_limit_bytes=48 * 1024 * 1024
        ),
        cost_estimate=pl.CostEstimate(
            flops=2 * rows * voxels * frames * 3,
            transcendentals=0,
            bytes_accessed=4 * (rows * voxels + 2 * frames * voxels + rows * frames),
        ),
    )(block, weighted, image, system)


def local(system, measured, row_class, band_weight, order):
    cycle_size = lax.axis_size("row")
    position = lax.axis_index("row")
    rows_here = system.shape[0]
    voxels = system.shape[1]
    subblocks = order.shape[1]
    subblock_rows = rows_here // subblocks
    band_hits = (
        row_class[:, None] == jnp.arange(band_weight.shape[0], dtype=jnp.int32)[None, :]
    ).astype(jnp.float32)
    row_weight = jnp.dot(band_hits, band_weight, precision=lax.Precision.HIGHEST) / (
        jnp.sum(system * system, axis=1) + epsilon
    )
    sequence = order[0]
    ordered = []
    for which in range(subblocks):
        first_row = sequence[which] * subblock_rows
        ordered.append(
            (
                sequence[which:which + 1],
                lax.dynamic_slice_in_dim(row_weight, first_row, subblock_rows, 0),
                first_row,
            )
        )
    particle_image = jnp.zeros((BATCH_FRAMES, voxels), jnp.float32)
    for visit_no in range(STEPS):
        frame_count = particle_image.shape[0]
        owner = (position - visit_no) % cycle_size
        first_frame = owner * BATCH_FRAMES
        for visit_which, (block, sub_weight, visit_first_row) in enumerate(ordered):
            observed_signal = lax.dynamic_slice(
                measured, (visit_first_row, first_frame), (subblock_rows, frame_count)
            )
            if visit_no == 0 and visit_which == 0:
                residual = observed_signal.T
            else:
                residual = (observed_signal - forward_t(particle_image, system, block, subblock_rows)).T
            particle_image = update(
                residual * sub_weight[None, :], particle_image, system, block, subblock_rows
            )
        if visit_no + 1 < STEPS:
            particle_image = shifted(particle_image, "row", 1)
    return shifted(particle_image, "row", 1 - STEPS)


def solution(mesh):
    return jax.shard_map(
        local,
        mesh=mesh,
        in_specs=(
            P(("grp", "row"), None),
            P(("grp", "row"), None),
            P(("grp", "row")),
            P("grp"),
            P(("grp", "row"), None),
        ),
        out_specs=P(("grp", "row"), None),
        check_vma=False,
    )
```

```python
import jax
import jax.numpy as jnp
from jax import lax
from jax.experimental import pallas as pl
from jax.experimental.pallas import tpu as pltpu
from jax.sharding import PartitionSpec as P

BATCH_FRAMES = 32
STEPS = 6
CHUNKS = 4


epsilon = 1e-06


def shifted(value, axis, steps):
    count = lax.axis_size(axis)
    pairs = [(source, (source + steps) % count) for source in range(count)]
    return lax.ppermute(value, axis, pairs)


TILE = 2048
_DN = (((1,), (1,)), ((), ()))


def _split(value):
    high = value.astype(jnp.bfloat16)
    return high, (value - high.astype(jnp.float32)).astype(jnp.bfloat16)


def _forward_kernel(offset_ref, image_ref, matrix_ref, total_ref, out_ref):
    @pl.when(pl.program_id(0) == 0)
    def _():
        out_ref[...] = total_ref[...]

    frames = image_ref.shape[0]
    image_hi, image_lo = _split(image_ref[...])
    both = jnp.concatenate([image_hi, image_lo], axis=0)
    matrix_hi, matrix_lo = _split(matrix_ref[...])
    paired = lax.dot_general(matrix_hi, both, _DN, preferred_element_type=jnp.float32)
    cross = lax.dot_general(matrix_lo, image_hi, _DN, preferred_element_type=jnp.float32)
    out_ref[...] += paired[:, :frames] + paired[:, frames:] + cross


def forward_t(image, system, block, rows, total, first):
    frames, width = image.shape
    tile = min(TILE, width)
    where = jnp.concatenate([block, jnp.full((1,), first // tile, jnp.int32)])
    return pl.pallas_call(
        _forward_kernel,
        out_shape=jax.ShapeDtypeStruct((rows, frames), jnp.float32),
        grid_spec=pltpu.PrefetchScalarGridSpec(
            num_scalar_prefetch=1,
            grid=(width // tile,),
            in_specs=[
                pl.BlockSpec((frames, tile), lambda j, off: (0, j)),
                pl.BlockSpec((rows, tile), lambda j, off: (off[0], off[1] + j)),
                pl.BlockSpec((rows, frames), lambda j, off: (0, 0)),
            ],
            out_specs=pl.BlockSpec((rows, frames), lambda j, off: (0, 0)),
        ),
        input_output_aliases={3: 0},
        compiler_params=pltpu.CompilerParams(
            dimension_semantics=("arbitrary",), vmem_limit_bytes=48 * 1024 * 1024
        ),
        cost_estimate=pl.CostEstimate(
            flops=2 * rows * width * frames * 3,
            transcendentals=0,
            bytes_accessed=4 * (rows * width + frames * width + 2 * rows * frames),
        ),
    )(where, image, system, total)


def _update_kernel(offset_ref, weighted_ref, image_ref, matrix_ref, out_ref):
    frames = image_ref.shape[0]
    weighted_hi, weighted_lo = _split(weighted_ref[...])
    both = jnp.concatenate([weighted_hi, weighted_lo], axis=0)
    matrix_hi, matrix_lo = _split(matrix_ref[...])
    paired = jnp.dot(both, matrix_hi, preferred_element_type=jnp.float32)
    cross = jnp.dot(weighted_hi, matrix_lo, preferred_element_type=jnp.float32)
    out_ref[...] = jnp.maximum(
        image_ref[...] + (paired[:frames] + paired[frames:] + cross), 0.0
    )


def update(weighted, image, system, block, rows, first, width):
    frames = image.shape[0]
    tile = min(TILE, width)
    chunked = image.shape[1] != width
    where = jnp.concatenate([block, jnp.full((1,), first // tile, jnp.int32)])
    return pl.pallas_call(
        _update_kernel,
        out_shape=jax.ShapeDtypeStruct((frames, width), jnp.float32),
        grid_spec=pltpu.PrefetchScalarGridSpec(
            num_scalar_prefetch=1,
            grid=(width // tile,),
            in_specs=[
                pl.BlockSpec((frames, rows), lambda j, off: (0, 0)),
                pl.BlockSpec((frames, tile), lambda j, off: (0, off[1] * chunked + j)),
                pl.BlockSpec((rows, tile), lambda j, off: (off[0], off[1] + j)),
            ],
            out_specs=pl.BlockSpec((frames, tile), lambda j, off: (0, j)),
        ),
        compiler_params=pltpu.CompilerParams(
            dimension_semantics=("arbitrary",), vmem_limit_bytes=48 * 1024 * 1024
        ),
        cost_estimate=pl.CostEstimate(
            flops=2 * rows * width * frames * 3,
            transcendentals=0,
            bytes_accessed=4 * (rows * width + 2 * frames * width + rows * frames),
        ),
    )(where, weighted, image, system)


def local(system, measured, row_class, band_weight, order):
    cycle_size = lax.axis_size("row")
    position = lax.axis_index("row")
    rows_here = system.shape[0]
    voxels = system.shape[1]
    subblocks = order.shape[1]
    subblock_rows = rows_here // subblocks
    band_hits = (
        row_class[:, None] == jnp.arange(band_weight.shape[0], dtype=jnp.int32)[None, :]
    ).astype(jnp.float32)
    row_weight = jnp.dot(band_hits, band_weight, precision=lax.Precision.HIGHEST) / (
        jnp.sum(system * system, axis=1) + epsilon
    )
    sequence = order[0]
    ordered = []
    for which in range(subblocks):
        first_row = sequence[which] * subblock_rows
        ordered.append(
            (
                sequence[which:which + 1],
                lax.dynamic_slice_in_dim(row_weight, first_row, subblock_rows, 0),
                first_row,
            )
        )
    width = voxels // CHUNKS
    chunks = [jnp.zeros((BATCH_FRAMES, width), jnp.float32) for _ in range(CHUNKS)]
    for visit_no in range(STEPS):
        owner = (position - visit_no) % cycle_size
        first_frame = owner * BATCH_FRAMES
        (block0, weight0, row0), (block1, weight1, row1) = ordered
        signal0 = lax.dynamic_slice(measured, (row0, first_frame), (subblock_rows, BATCH_FRAMES))
        signal1 = lax.dynamic_slice(measured, (row1, first_frame), (subblock_rows, BATCH_FRAMES))
        if visit_no == 0:
            residual = signal0.T
        else:
            total = jnp.zeros((subblock_rows, BATCH_FRAMES), jnp.float32)
            for index, chunk in enumerate(chunks):
                total = forward_t(chunk, system, block0, subblock_rows, total, index * width)
            residual = (signal0 - total).T
        image = jnp.concatenate(chunks, axis=1)
        image = update(residual * weight0[None, :], image, system, block0, subblock_rows, 0, voxels)
        total = jnp.zeros((subblock_rows, BATCH_FRAMES), jnp.float32)
        total = forward_t(image, system, block1, subblock_rows, total, 0)
        weighted = (signal1 - total).T * weight1[None, :]
        steps = 1 if visit_no + 1 < STEPS else 1 - STEPS
        chunks = [
            shifted(
                update(weighted, image, system, block1, subblock_rows, index * width, width),
                "row",
                steps,
            )
            for index in range(CHUNKS)
        ]
    return jnp.concatenate(chunks, axis=1)


def solution(mesh):
    return jax.shard_map(
        local,
        mesh=mesh,
        in_specs=(
            P(("grp", "row"), None),
            P(("grp", "row"), None),
            P(("grp", "row")),
            P("grp"),
            P(("grp", "row"), None),
        ),
        out_specs=P(("grp", "row"), None),
        check_vma=False,
    )
```

```python
import jax
import numpy as np
import jax.numpy as jnp
from jax import lax
from jax.experimental import pallas as pl
from jax.experimental.pallas import tpu as pltpu
from jax.sharding import PartitionSpec as P

BATCH_FRAMES = 32
STEPS = 6
CHUNKS = 4


epsilon = 1e-06


def shifted(value, axis, steps):
    count = lax.axis_size(axis)
    pairs = [(source, (source + steps) % count) for source in range(count)]
    return lax.ppermute(value, axis, pairs)


TILE = 2048
_DN = (((1,), (1,)), ((), ()))


def _split(value):
    high = value.astype(jnp.bfloat16)
    return high, (value - high.astype(jnp.float32)).astype(jnp.bfloat16)


def _forward_kernel(offset_ref, start_ref, image_ref, matrix_ref, total_ref, out_ref):
    @pl.when(pl.program_id(0) == 0)
    def _():
        out_ref[...] = total_ref[...]

    frames = image_ref.shape[0]
    image_hi, image_lo = _split(image_ref[...])
    both = jnp.concatenate([image_hi, image_lo], axis=0)
    matrix_hi, matrix_lo = _split(matrix_ref[...])
    paired = lax.dot_general(matrix_hi, both, _DN, preferred_element_type=jnp.float32)
    cross = lax.dot_general(matrix_lo, image_hi, _DN, preferred_element_type=jnp.float32)
    out_ref[...] += paired[:, :frames] + paired[:, frames:] + cross


def forward_t(image, system, block, rows, total, first):
    frames, width = image.shape
    tile = min(TILE, width)
    start = np.array([first // tile], np.int32)
    return pl.pallas_call(
        _forward_kernel,
        out_shape=jax.ShapeDtypeStruct((rows, frames), jnp.float32),
        grid_spec=pltpu.PrefetchScalarGridSpec(
            num_scalar_prefetch=2,
            grid=(width // tile,),
            in_specs=[
                pl.BlockSpec((frames, tile), lambda j, off, st: (0, j)),
                pl.BlockSpec((rows, tile), lambda j, off, st: (off[0], st[0] + j)),
                pl.BlockSpec((rows, frames), lambda j, off, st: (0, 0)),
            ],
            out_specs=pl.BlockSpec((rows, frames), lambda j, off, st: (0, 0)),
        ),
        input_output_aliases={4: 0},
        compiler_params=pltpu.CompilerParams(
            dimension_semantics=("arbitrary",), vmem_limit_bytes=48 * 1024 * 1024
        ),
        cost_estimate=pl.CostEstimate(
            flops=2 * rows * width * frames * 3,
            transcendentals=0,
            bytes_accessed=4 * (rows * width + frames * width + 2 * rows * frames),
        ),
    )(block, start, image, system, total)


def _update_kernel(offset_ref, start_ref, weighted_ref, image_ref, matrix_ref, *rest):
    out_ref = rest[-1]
    frames = image_ref.shape[0]
    weighted_hi, weighted_lo = _split(weighted_ref[...])
    both = jnp.concatenate([weighted_hi, weighted_lo], axis=0)
    matrix_hi, matrix_lo = _split(matrix_ref[...])
    paired = jnp.dot(both, matrix_hi, preferred_element_type=jnp.float32)
    cross = jnp.dot(weighted_hi, matrix_lo, preferred_element_type=jnp.float32)
    out_ref[...] = jnp.maximum(
        image_ref[...] + (paired[:frames] + paired[frames:] + cross), 0.0
    )


def update(weighted, image, system, block, rows, first, width, after=None):
    frames = image.shape[0]
    tile = min(TILE, width)
    chunked = image.shape[1] != width
    start = np.array([first // tile], np.int32)
    extra_specs, extra = [], []
    if after is not None:
        extra_specs, extra = [pl.BlockSpec((8, 128), lambda j, off, st: (0, 0))], [after]
    return pl.pallas_call(
        _update_kernel,
        out_shape=jax.ShapeDtypeStruct((frames, width), jnp.float32),
        grid_spec=pltpu.PrefetchScalarGridSpec(
            num_scalar_prefetch=2,
            grid=(width // tile,),
            in_specs=[
                pl.BlockSpec((frames, rows), lambda j, off, st: (0, 0)),
                pl.BlockSpec((frames, tile), lambda j, off, st: (0, st[0] * chunked + j)),
                pl.BlockSpec((rows, tile), lambda j, off, st: (off[0], st[0] + j)),
            ]
            + extra_specs,
            out_specs=pl.BlockSpec((frames, tile), lambda j, off, st: (0, j)),
        ),
        compiler_params=pltpu.CompilerParams(
            dimension_semantics=("arbitrary",), vmem_limit_bytes=48 * 1024 * 1024
        ),
        cost_estimate=pl.CostEstimate(
            flops=2 * rows * width * frames * 3,
            transcendentals=0,
            bytes_accessed=4 * (rows * width + 2 * frames * width + rows * frames),
        ),
    )(block, start, weighted, image, system, *extra)


def local(system, measured, row_class, band_weight, order):
    cycle_size = lax.axis_size("row")
    position = lax.axis_index("row")
    rows_here = system.shape[0]
    voxels = system.shape[1]
    subblocks = order.shape[1]
    subblock_rows = rows_here // subblocks
    band_hits = (
        row_class[:, None] == jnp.arange(band_weight.shape[0], dtype=jnp.int32)[None, :]
    ).astype(jnp.float32)
    row_weight = jnp.dot(band_hits, band_weight, precision=lax.Precision.HIGHEST) / (
        jnp.sum(system * system, axis=1) + epsilon
    )
    sequence = order[0]
    ordered = []
    for which in range(subblocks):
        first_row = sequence[which] * subblock_rows
        ordered.append(
            (
                sequence[which:which + 1],
                lax.dynamic_slice_in_dim(row_weight, first_row, subblock_rows, 0),
                first_row,
            )
        )
    width = voxels // CHUNKS
    chunks = [jnp.zeros((BATCH_FRAMES, width), jnp.float32) for _ in range(CHUNKS)]
    for visit_no in range(STEPS):
        owner = (position - visit_no) % cycle_size
        first_frame = owner * BATCH_FRAMES
        (block0, weight0, row0), (block1, weight1, row1) = ordered
        signal0 = lax.dynamic_slice(measured, (row0, first_frame), (subblock_rows, BATCH_FRAMES))
        signal1 = lax.dynamic_slice(measured, (row1, first_frame), (subblock_rows, BATCH_FRAMES))
        if visit_no == 0:
            residual = signal0.T
        else:
            total = jnp.zeros((subblock_rows, BATCH_FRAMES), jnp.float32)
            for index, chunk in enumerate(chunks):
                total = forward_t(chunk, system, block0, subblock_rows, total, index * width)
            residual = (signal0 - total).T
        image = jnp.concatenate(chunks, axis=1)
        image = update(residual * weight0[None, :], image, system, block0, subblock_rows, 0, voxels)
        total = jnp.zeros((subblock_rows, BATCH_FRAMES), jnp.float32)
        total = forward_t(image, system, block1, subblock_rows, total, 0)
        weighted = (signal1 - total).T * weight1[None, :]
        steps = 1 if visit_no + 1 < STEPS else 1 - STEPS
        chunks = []
        for index in range(CHUNKS):
            after = chunks[index - 2] if visit_no + 1 == STEPS and index >= 2 else None
            piece = update(
                weighted, image, system, block1, subblock_rows, index * width, width, after
            )
            chunks.append(shifted(piece, "row", steps))
    return jnp.concatenate(chunks, axis=1)


def solution(mesh):
    return jax.shard_map(
        local,
        mesh=mesh,
        in_specs=(
            P(("grp", "row"), None),
            P(("grp", "row"), None),
            P(("grp", "row")),
            P("grp"),
            P(("grp", "row"), None),
        ),
        out_specs=P(("grp", "row"), None),
        check_vma=False,
    )
```

```python
import jax
import numpy as np
import jax.numpy as jnp
from jax import lax
from jax.experimental import pallas as pl
from jax.experimental.pallas import tpu as pltpu
from jax.sharding import PartitionSpec as P

BATCH_FRAMES = 32
STEPS = 6
CHUNKS = 4


epsilon = 1e-06


def shifted(value, axis, steps):
    count = lax.axis_size(axis)
    pairs = [(source, (source + steps) % count) for source in range(count)]
    return lax.ppermute(value, axis, pairs)


TILE = 4096
_DN = (((1,), (1,)), ((), ()))


def _split(value):
    high = value.astype(jnp.bfloat16)
    return high, (value - high.astype(jnp.float32)).astype(jnp.bfloat16)


def _forward_kernel(offset_ref, start_ref, image_ref, matrix_ref, *rest):
    out_ref = rest[-1]

    @pl.when(pl.program_id(0) == 0)
    def _():
        if len(rest) == 2:
            out_ref[...] = rest[0][...]
        else:
            out_ref[...] = jnp.zeros_like(out_ref)

    frames = image_ref.shape[0]
    image_hi, image_lo = _split(image_ref[...])
    both = jnp.concatenate([image_hi, image_lo], axis=0)
    matrix_hi, matrix_lo = _split(matrix_ref[...])
    paired = lax.dot_general(matrix_hi, both, _DN, preferred_element_type=jnp.float32)
    cross = lax.dot_general(matrix_lo, image_hi, _DN, preferred_element_type=jnp.float32)
    out_ref[...] += paired[:, :frames] + paired[:, frames:] + cross


def forward_t(image, system, block, rows, total, first):
    frames, width = image.shape
    tile = min(TILE, width // 2)
    start = np.array([first // tile], np.int32)
    operands, specs, aliases = [block, start, image, system], [], {}
    if total is not None:
        operands.append(total)
        specs = [pl.BlockSpec((rows, frames), lambda j, off, st: (0, 0))]
        aliases = {4: 0}
    return pl.pallas_call(
        _forward_kernel,
        out_shape=jax.ShapeDtypeStruct((rows, frames), jnp.float32),
        grid_spec=pltpu.PrefetchScalarGridSpec(
            num_scalar_prefetch=2,
            grid=(width // tile,),
            in_specs=[
                pl.BlockSpec((frames, tile), lambda j, off, st: (0, j)),
                pl.BlockSpec((rows, tile), lambda j, off, st: (off[0], st[0] + j)),
            ]
            + specs,
            out_specs=pl.BlockSpec((rows, frames), lambda j, off, st: (0, 0)),
        ),
        input_output_aliases=aliases,
        compiler_params=pltpu.CompilerParams(
            dimension_semantics=("arbitrary",), vmem_limit_bytes=48 * 1024 * 1024
        ),
        cost_estimate=pl.CostEstimate(
            flops=2 * rows * width * frames * 3,
            transcendentals=0,
            bytes_accessed=4 * (rows * width + frames * width + 2 * rows * frames),
        ),
    )(*operands)


def _update_kernel(offset_ref, start_ref, weighted_ref, image_ref, matrix_ref, *rest):
    out_ref = rest[-1]
    frames = image_ref.shape[0]
    weighted_hi, weighted_lo = _split(weighted_ref[...])
    both = jnp.concatenate([weighted_hi, weighted_lo], axis=0)
    matrix_hi, matrix_lo = _split(matrix_ref[...])
    paired = jnp.dot(both, matrix_hi, preferred_element_type=jnp.float32)
    cross = jnp.dot(weighted_hi, matrix_lo, preferred_element_type=jnp.float32)
    out_ref[...] = jnp.maximum(
        image_ref[...] + (paired[:frames] + paired[frames:] + cross), 0.0
    )


def update(weighted, image, system, block, rows, first, width, after=None):
    frames = image.shape[0]
    tile = min(TILE, width // 2)
    chunked = image.shape[1] != width
    start = np.array([first // tile], np.int32)
    extra_specs, extra = [], []
    if after is not None:
        extra_specs, extra = [pl.BlockSpec((8, 128), lambda j, off, st: (0, 0))], [after]
    return pl.pallas_call(
        _update_kernel,
        out_shape=jax.ShapeDtypeStruct((frames, width), jnp.float32),
        grid_spec=pltpu.PrefetchScalarGridSpec(
            num_scalar_prefetch=2,
            grid=(width // tile,),
            in_specs=[
                pl.BlockSpec((frames, rows), lambda j, off, st: (0, 0)),
                pl.BlockSpec((frames, tile), lambda j, off, st: (0, st[0] * chunked + j)),
                pl.BlockSpec((rows, tile), lambda j, off, st: (off[0], st[0] + j)),
            ]
            + extra_specs,
            out_specs=pl.BlockSpec((frames, tile), lambda j, off, st: (0, j)),
        ),
        compiler_params=pltpu.CompilerParams(
            dimension_semantics=("arbitrary",), vmem_limit_bytes=48 * 1024 * 1024
        ),
        cost_estimate=pl.CostEstimate(
            flops=2 * rows * width * frames * 3,
            transcendentals=0,
            bytes_accessed=4 * (rows * width + 2 * frames * width + rows * frames),
        ),
    )(block, start, weighted, image, system, *extra)


def local(system, measured, row_class, band_weight, order):
    cycle_size = lax.axis_size("row")
    position = lax.axis_index("row")
    rows_here = system.shape[0]
    voxels = system.shape[1]
    subblocks = order.shape[1]
    subblock_rows = rows_here // subblocks
    band_hits = (
        row_class[:, None] == jnp.arange(band_weight.shape[0], dtype=jnp.int32)[None, :]
    ).astype(jnp.float32)
    row_weight = jnp.dot(band_hits, band_weight, precision=lax.Precision.HIGHEST) / (
        jnp.sum(system * system, axis=1) + epsilon
    )
    sequence = order[0]
    ordered = []
    for which in range(subblocks):
        first_row = sequence[which] * subblock_rows
        ordered.append(
            (
                sequence[which:which + 1],
                lax.dynamic_slice_in_dim(row_weight, first_row, subblock_rows, 0),
                first_row,
            )
        )
    width = voxels // CHUNKS
    chunks = [jnp.zeros((BATCH_FRAMES, width), jnp.float32) for _ in range(CHUNKS)]
    for visit_no in range(STEPS):
        owner = (position - visit_no) % cycle_size
        first_frame = owner * BATCH_FRAMES
        (block0, weight0, row0), (block1, weight1, row1) = ordered
        signal0 = lax.dynamic_slice(measured, (row0, first_frame), (subblock_rows, BATCH_FRAMES))
        signal1 = lax.dynamic_slice(measured, (row1, first_frame), (subblock_rows, BATCH_FRAMES))
        if visit_no == 0:
            residual = signal0.T
        else:
            total = None
            for index, chunk in enumerate(chunks):
                total = forward_t(chunk, system, block0, subblock_rows, total, index * width)
            residual = (signal0 - total).T
        image = jnp.concatenate(chunks, axis=1)
        image = update(residual * weight0[None, :], image, system, block0, subblock_rows, 0, voxels)
        total = forward_t(image, system, block1, subblock_rows, None, 0)
        weighted = (signal1 - total).T * weight1[None, :]
        steps = 1 if visit_no + 1 < STEPS else 1 - STEPS
        chunks = []
        for index in range(CHUNKS):
            after = chunks[index - 2] if visit_no + 1 == STEPS and index >= 2 else None
            piece = update(
                weighted, image, system, block1, subblock_rows, index * width, width, after
            )
            chunks.append(shifted(piece, "row", steps))
    return jnp.concatenate(chunks, axis=1)


def solution(mesh):
    return jax.shard_map(
        local,
        mesh=mesh,
        in_specs=(
            P(("grp", "row"), None),
            P(("grp", "row"), None),
            P(("grp", "row")),
            P("grp"),
            P(("grp", "row"), None),
        ),
        out_specs=P(("grp", "row"), None),
        check_vma=False,
    )
```

```python
import jax
import numpy as np
import jax.numpy as jnp
from jax import lax
from jax.experimental import pallas as pl
from jax.experimental.pallas import tpu as pltpu
from jax.sharding import PartitionSpec as P

BATCH_FRAMES = 32
STEPS = 6
CHUNKS = 4


epsilon = 1e-06


def shifted(value, axis, steps):
    count = lax.axis_size(axis)
    pairs = [(source, (source + steps) % count) for source in range(count)]
    return lax.ppermute(value, axis, pairs)


TILE = 4096
_DN = (((1,), (1,)), ((), ()))


def _split(value):
    high = value.astype(jnp.bfloat16)
    return high, (value - high.astype(jnp.float32)).astype(jnp.bfloat16)


def _forward_kernel(offset_ref, start_ref, image_ref, matrix_ref, *rest):
    out_ref = rest[-1]

    @pl.when(pl.program_id(0) == 0)
    def _():
        if len(rest) == 2:
            out_ref[...] = rest[0][...]
        else:
            out_ref[...] = jnp.zeros_like(out_ref)

    frames = image_ref.shape[0]
    image_hi, image_lo = _split(image_ref[...])
    both = jnp.concatenate([image_hi, image_lo], axis=0)
    matrix_hi, matrix_lo = _split(matrix_ref[...])
    paired = lax.dot_general(matrix_hi, both, _DN, preferred_element_type=jnp.float32)
    cross = lax.dot_general(matrix_lo, image_hi, _DN, preferred_element_type=jnp.float32)
    out_ref[...] += paired[:, :frames] + paired[:, frames:] + cross


def forward_t(image, system, block, rows, total, first):
    frames, width = image.shape
    tile = min(TILE, width // 2)
    start = np.array([first // tile], np.int32)
    operands, specs, aliases = [block, start, image, system], [], {}
    if total is not None:
        operands.append(total)
        specs = [pl.BlockSpec((rows, frames), lambda j, off, st: (0, 0))]
        aliases = {4: 0}
    return pl.pallas_call(
        _forward_kernel,
        out_shape=jax.ShapeDtypeStruct((rows, frames), jnp.float32),
        grid_spec=pltpu.PrefetchScalarGridSpec(
            num_scalar_prefetch=2,
            grid=(width // tile,),
            in_specs=[
                pl.BlockSpec((frames, tile), lambda j, off, st: (0, j)),
                pl.BlockSpec((rows, tile), lambda j, off, st: (off[0], st[0] + j)),
            ]
            + specs,
            out_specs=pl.BlockSpec((rows, frames), lambda j, off, st: (0, 0)),
        ),
        input_output_aliases=aliases,
        compiler_params=pltpu.CompilerParams(
            dimension_semantics=("arbitrary",), vmem_limit_bytes=48 * 1024 * 1024
        ),
        cost_estimate=pl.CostEstimate(
            flops=2 * rows * width * frames * 3,
            transcendentals=0,
            bytes_accessed=4 * (rows * width + frames * width + 2 * rows * frames),
        ),
    )(*operands)


def _update_kernel(offset_ref, start_ref, weighted_ref, image_ref, matrix_ref, *rest):
    out_ref = rest[-1]
    frames = image_ref.shape[0]
    weighted_hi, weighted_lo = _split(weighted_ref[...])
    both = jnp.concatenate([weighted_hi, weighted_lo], axis=0)
    matrix_hi, matrix_lo = _split(matrix_ref[...])
    paired = jnp.dot(both, matrix_hi, preferred_element_type=jnp.float32)
    cross = jnp.dot(weighted_hi, matrix_lo, preferred_element_type=jnp.float32)
    out_ref[...] = jnp.maximum(
        image_ref[...] + (paired[:frames] + paired[frames:] + cross), 0.0
    )


def update(weighted, image, system, block, rows, first, width, after=None):
    frames = image.shape[0]
    tile = min(TILE, width // 2)
    chunked = image.shape[1] != width
    start = np.array([first // tile], np.int32)
    extra_specs, extra = [], []
    if after is not None:
        block_shape = (8, min(128, after.shape[1]))
        extra_specs, extra = [pl.BlockSpec(block_shape, lambda j, off, st: (0, 0))], [after]
    return pl.pallas_call(
        _update_kernel,
        out_shape=jax.ShapeDtypeStruct((frames, width), jnp.float32),
        grid_spec=pltpu.PrefetchScalarGridSpec(
            num_scalar_prefetch=2,
            grid=(width // tile,),
            in_specs=[
                pl.BlockSpec((frames, rows), lambda j, off, st: (0, 0)),
                pl.BlockSpec((frames, tile), lambda j, off, st: (0, st[0] * chunked + j)),
                pl.BlockSpec((rows, tile), lambda j, off, st: (off[0], st[0] + j)),
            ]
            + extra_specs,
            out_specs=pl.BlockSpec((frames, tile), lambda j, off, st: (0, j)),
        ),
        compiler_params=pltpu.CompilerParams(
            dimension_semantics=("arbitrary",), vmem_limit_bytes=48 * 1024 * 1024
        ),
        cost_estimate=pl.CostEstimate(
            flops=2 * rows * width * frames * 3,
            transcendentals=0,
            bytes_accessed=4 * (rows * width + 2 * frames * width + rows * frames),
        ),
    )(block, start, weighted, image, system, *extra)


def local(system, measured, row_class, band_weight, order):
    cycle_size = lax.axis_size("row")
    position = lax.axis_index("row")
    rows_here = system.shape[0]
    voxels = system.shape[1]
    subblocks = order.shape[1]
    subblock_rows = rows_here // subblocks
    band_hits = (
        row_class[:, None] == jnp.arange(band_weight.shape[0], dtype=jnp.int32)[None, :]
    ).astype(jnp.float32)
    row_weight = jnp.dot(band_hits, band_weight, precision=lax.Precision.HIGHEST) / (
        jnp.sum(system * system, axis=1) + epsilon
    )
    sequence = order[0]
    ordered = []
    for which in range(subblocks):
        first_row = sequence[which] * subblock_rows
        ordered.append(
            (
                sequence[which:which + 1],
                lax.dynamic_slice_in_dim(row_weight, first_row, subblock_rows, 0),
                first_row,
            )
        )
    width = voxels // CHUNKS
    chunks = [jnp.zeros((BATCH_FRAMES, width), jnp.float32) for _ in range(CHUNKS)]
    head = None
    for visit_no in range(STEPS):
        owner = (position - visit_no) % cycle_size
        first_frame = owner * BATCH_FRAMES
        (block0, weight0, row0), (block1, weight1, row1) = ordered
        signal0 = lax.dynamic_slice(measured, (row0, first_frame), (subblock_rows, BATCH_FRAMES))
        signal1 = lax.dynamic_slice(measured, (row1, first_frame), (subblock_rows, BATCH_FRAMES))
        if visit_no == 0:
            residual = signal0.T
        else:
            total = head
            for index in range(1, CHUNKS):
                total = forward_t(chunks[index], system, block0, subblock_rows, total, index * width)
            residual = (signal0 - total).T
        image = jnp.concatenate(chunks, axis=1)
        image = update(residual * weight0[None, :], image, system, block0, subblock_rows, 0, voxels)
        total = forward_t(image, system, block1, subblock_rows, None, 0)
        weighted = (signal1 - total).T * weight1[None, :]
        last = visit_no + 1 == STEPS
        steps = 1 if not last else 1 - STEPS
        chunks = []
        for index in range(CHUNKS):
            after = None
            if last and index >= 2:
                after = chunks[index - 2]
            elif not last and index == CHUNKS - 1:
                head = forward_t(chunks[0], system, block0, subblock_rows, None, 0)
                after = head
            piece = update(
                weighted, image, system, block1, subblock_rows, index * width, width, after
            )
            chunks.append(shifted(piece, "row", steps))
    return jnp.concatenate(chunks, axis=1)


def solution(mesh):
    return jax.shard_map(
        local,
        mesh=mesh,
        in_specs=(
            P(("grp", "row"), None),
            P(("grp", "row"), None),
            P(("grp", "row")),
            P("grp"),
            P(("grp", "row"), None),
        ),
        out_specs=P(("grp", "row"), None),
        check_vma=False,
    )
```

```python
import functools

import jax
import numpy as np
import jax.numpy as jnp
from jax import lax
from jax.experimental import pallas as pl
from jax.experimental.pallas import tpu as pltpu
from jax.sharding import PartitionSpec as P

BATCH_FRAMES = 32
STEPS = 6
CHUNKS = 4


epsilon = 1e-06


def shifted(value, axis, steps):
    count = lax.axis_size(axis)
    pairs = [(source, (source + steps) % count) for source in range(count)]
    return lax.ppermute(value, axis, pairs)


TILE = 4096
_DN = (((1,), (1,)), ((), ()))


def _split(value):
    high = value.astype(jnp.bfloat16)
    return high, (value - high.astype(jnp.float32)).astype(jnp.bfloat16)


def _forward_kernel(with_total, with_norms, offset_ref, start_ref, image_ref, matrix_ref, *rest):
    out_ref = rest[1] if with_total else rest[0]
    norm_ref = rest[-1] if with_norms else None

    @pl.when(pl.program_id(0) == 0)
    def _():
        if with_total:
            out_ref[...] = rest[0][...]
        else:
            out_ref[...] = jnp.zeros_like(out_ref)
        if with_norms:
            norm_ref[...] = jnp.zeros_like(norm_ref)

    if with_norms:
        square = matrix_ref[...] * matrix_ref[...]
        norm_ref[...] += jnp.sum(square, axis=1, keepdims=True)

    frames = image_ref.shape[0]
    image_hi, image_lo = _split(image_ref[...])
    both = jnp.concatenate([image_hi, image_lo], axis=0)
    matrix_hi, matrix_lo = _split(matrix_ref[...])
    paired = lax.dot_general(matrix_hi, both, _DN, preferred_element_type=jnp.float32)
    cross = lax.dot_general(matrix_lo, image_hi, _DN, preferred_element_type=jnp.float32)
    out_ref[...] += paired[:, :frames] + paired[:, frames:] + cross


def forward_t(image, system, block, rows, total, first, norms=False):
    frames, width = image.shape
    tile = min(TILE, width // 2)
    start = np.array([first // tile], np.int32)
    operands, specs, aliases = [block, start, image, system], [], {}
    if total is not None:
        operands.append(total)
        specs = [pl.BlockSpec((rows, frames), lambda j, off, st: (0, 0))]
        aliases = {4: 0}
    out_shape = [jax.ShapeDtypeStruct((rows, frames), jnp.float32)]
    out_specs = [pl.BlockSpec((rows, frames), lambda j, off, st: (0, 0))]
    if norms:
        out_shape.append(jax.ShapeDtypeStruct((rows, 1), jnp.float32))
        out_specs.append(pl.BlockSpec((rows, 1), lambda j, off, st: (0, 0)))
    result = pl.pallas_call(
        functools.partial(_forward_kernel, total is not None, norms),
        out_shape=out_shape,
        grid_spec=pltpu.PrefetchScalarGridSpec(
            num_scalar_prefetch=2,
            grid=(width // tile,),
            in_specs=[
                pl.BlockSpec((frames, tile), lambda j, off, st: (0, j)),
                pl.BlockSpec((rows, tile), lambda j, off, st: (off[0], st[0] + j)),
            ]
            + specs,
            out_specs=out_specs,
        ),
        input_output_aliases=aliases,
        compiler_params=pltpu.CompilerParams(
            dimension_semantics=("arbitrary",), vmem_limit_bytes=48 * 1024 * 1024
        ),
        cost_estimate=pl.CostEstimate(
            flops=2 * rows * width * frames * 3,
            transcendentals=0,
            bytes_accessed=4 * (rows * width + frames * width + 2 * rows * frames),
        ),
    )(*operands)
    return result if norms else result[0]


def _update_kernel(offset_ref, start_ref, weighted_ref, image_ref, matrix_ref, *rest):
    out_ref = rest[-1]
    frames = image_ref.shape[0]
    weighted_hi, weighted_lo = _split(weighted_ref[...])
    both = jnp.concatenate([weighted_hi, weighted_lo], axis=0)
    matrix_hi, matrix_lo = _split(matrix_ref[...])
    paired = jnp.dot(both, matrix_hi, preferred_element_type=jnp.float32)
    cross = jnp.dot(weighted_hi, matrix_lo, preferred_element_type=jnp.float32)
    out_ref[...] = jnp.maximum(
        image_ref[...] + (paired[:frames] + paired[frames:] + cross), 0.0
    )


def update(weighted, image, system, block, rows, first, width, after=None):
    frames = image.shape[0]
    tile = min(TILE, width // 2)
    chunked = image.shape[1] != width
    start = np.array([first // tile], np.int32)
    extra_specs, extra = [], []
    if after is not None:
        block_shape = (8, min(128, after.shape[1]))
        extra_specs, extra = [pl.BlockSpec(block_shape, lambda j, off, st: (0, 0))], [after]
    return pl.pallas_call(
        _update_kernel,
        out_shape=jax.ShapeDtypeStruct((frames, width), jnp.float32),
        grid_spec=pltpu.PrefetchScalarGridSpec(
            num_scalar_prefetch=2,
            grid=(width // tile,),
            in_specs=[
                pl.BlockSpec((frames, rows), lambda j, off, st: (0, 0)),
                pl.BlockSpec((frames, tile), lambda j, off, st: (0, st[0] * chunked + j)),
                pl.BlockSpec((rows, tile), lambda j, off, st: (off[0], st[0] + j)),
            ]
            + extra_specs,
            out_specs=pl.BlockSpec((frames, tile), lambda j, off, st: (0, j)),
        ),
        compiler_params=pltpu.CompilerParams(
            dimension_semantics=("arbitrary",), vmem_limit_bytes=48 * 1024 * 1024
        ),
        cost_estimate=pl.CostEstimate(
            flops=2 * rows * width * frames * 3,
            transcendentals=0,
            bytes_accessed=4 * (rows * width + 2 * frames * width + rows * frames),
        ),
    )(block, start, weighted, image, system, *extra)


def local(system, measured, row_class, band_weight, order):
    cycle_size = lax.axis_size("row")
    position = lax.axis_index("row")
    rows_here = system.shape[0]
    voxels = system.shape[1]
    subblocks = order.shape[1]
    subblock_rows = rows_here // subblocks
    band_hits = (
        row_class[:, None] == jnp.arange(band_weight.shape[0], dtype=jnp.int32)[None, :]
    ).astype(jnp.float32)
    band = jnp.dot(band_hits, band_weight, precision=lax.Precision.HIGHEST)
    sequence = order[0]
    ordered = []
    for which in range(subblocks):
        first_row = sequence[which] * subblock_rows
        ordered.append(
            (
                sequence[which:which + 1],
                lax.dynamic_slice_in_dim(band, first_row, subblock_rows, 0),
                first_row,
            )
        )
    first_rows = lax.dynamic_slice_in_dim(system, ordered[0][2], subblock_rows, 0)
    weight0 = ordered[0][1] / (jnp.sum(first_rows * first_rows, axis=1) + epsilon)
    width = voxels // CHUNKS
    chunks = [jnp.zeros((BATCH_FRAMES, width), jnp.float32) for _ in range(CHUNKS)]
    head = None
    for visit_no in range(STEPS):
        owner = (position - visit_no) % cycle_size
        first_frame = owner * BATCH_FRAMES
        (block0, _, row0), (block1, band1, row1) = ordered
        signal0 = lax.dynamic_slice(measured, (row0, first_frame), (subblock_rows, BATCH_FRAMES))
        signal1 = lax.dynamic_slice(measured, (row1, first_frame), (subblock_rows, BATCH_FRAMES))
        if visit_no == 0:
            residual = signal0.T
        else:
            total = head
            for index in range(1, CHUNKS):
                total = forward_t(chunks[index], system, block0, subblock_rows, total, index * width)
            residual = (signal0 - total).T
        image = jnp.concatenate(chunks, axis=1)
        image = update(residual * weight0[None, :], image, system, block0, subblock_rows, 0, voxels)
        if visit_no == 0:
            total, norms = forward_t(image, system, block1, subblock_rows, None, 0, True)
            weight1 = band1 / (norms[:, 0] + epsilon)
        else:
            total = forward_t(image, system, block1, subblock_rows, None, 0)
        weighted = (signal1 - total).T * weight1[None, :]
        last = visit_no + 1 == STEPS
        steps = 1 if not last else 1 - STEPS
        chunks = []
        for index in range(CHUNKS):
            after = None
            if last and index >= 2:
                after = chunks[index - 2]
            elif not last and index == CHUNKS - 1:
                head = forward_t(chunks[0], system, block0, subblock_rows, None, 0)
                after = head
            piece = update(
                weighted, image, system, block1, subblock_rows, index * width, width, after
            )
            chunks.append(shifted(piece, "row", steps))
    return jnp.concatenate(chunks, axis=1)


def solution(mesh):
    return jax.shard_map(
        local,
        mesh=mesh,
        in_specs=(
            P(("grp", "row"), None),
            P(("grp", "row"), None),
            P(("grp", "row")),
            P("grp"),
            P(("grp", "row"), None),
        ),
        out_specs=P(("grp", "row"), None),
        check_vma=False,
    )
```

```python
import functools

import jax
import numpy as np
import jax.numpy as jnp
from jax import lax
from jax.experimental import pallas as pl
from jax.experimental.pallas import tpu as pltpu
from jax.sharding import PartitionSpec as P

BATCH_FRAMES = 32
STEPS = 6
CHUNKS = 4


epsilon = 1e-06


def shifted(value, axis, steps):
    count = lax.axis_size(axis)
    pairs = [(source, (source + steps) % count) for source in range(count)]
    return lax.ppermute(value, axis, pairs)


TILE = 4096
MIDDLE_TILE = 2048
_DN = (((1,), (1,)), ((), ()))


def _split(value):
    high = value.astype(jnp.bfloat16)
    return high, (value - high.astype(jnp.float32)).astype(jnp.bfloat16)


def _forward_kernel(with_total, with_norms, offset_ref, start_ref, image_ref, matrix_ref, *rest):
    out_ref = rest[1] if with_total else rest[0]
    norm_ref = rest[-1] if with_norms else None

    @pl.when(pl.program_id(0) == 0)
    def _():
        if with_total:
            out_ref[...] = rest[0][...]
        else:
            out_ref[...] = jnp.zeros_like(out_ref)
        if with_norms:
            norm_ref[...] = jnp.zeros_like(norm_ref)

    if with_norms:
        square = matrix_ref[...] * matrix_ref[...]
        norm_ref[...] += jnp.sum(square, axis=1, keepdims=True)

    frames = image_ref.shape[0]
    image_hi, image_lo = _split(image_ref[...])
    both = jnp.concatenate([image_hi, image_lo], axis=0)
    matrix_hi, matrix_lo = _split(matrix_ref[...])
    paired = lax.dot_general(matrix_hi, both, _DN, preferred_element_type=jnp.float32)
    cross = lax.dot_general(matrix_lo, image_hi, _DN, preferred_element_type=jnp.float32)
    out_ref[...] += paired[:, :frames] + paired[:, frames:] + cross


def forward_t(image, system, block, rows, total, first, norms=False):
    frames, width = image.shape
    tile = min(TILE, width // 2)
    start = np.array([first // tile], np.int32)
    operands, specs, aliases = [block, start, image, system], [], {}
    if total is not None:
        operands.append(total)
        specs = [pl.BlockSpec((rows, frames), lambda j, off, st: (0, 0))]
        aliases = {4: 0}
    out_shape = [jax.ShapeDtypeStruct((rows, frames), jnp.float32)]
    out_specs = [pl.BlockSpec((rows, frames), lambda j, off, st: (0, 0))]
    if norms:
        out_shape.append(jax.ShapeDtypeStruct((rows, 1), jnp.float32))
        out_specs.append(pl.BlockSpec((rows, 1), lambda j, off, st: (0, 0)))
    result = pl.pallas_call(
        functools.partial(_forward_kernel, total is not None, norms),
        out_shape=out_shape,
        grid_spec=pltpu.PrefetchScalarGridSpec(
            num_scalar_prefetch=2,
            grid=(width // tile,),
            in_specs=[
                pl.BlockSpec((frames, tile), lambda j, off, st: (0, j)),
                pl.BlockSpec((rows, tile), lambda j, off, st: (off[0], st[0] + j)),
            ]
            + specs,
            out_specs=out_specs,
        ),
        input_output_aliases=aliases,
        compiler_params=pltpu.CompilerParams(
            dimension_semantics=("arbitrary",), vmem_limit_bytes=48 * 1024 * 1024
        ),
        cost_estimate=pl.CostEstimate(
            flops=2 * rows * width * frames * 3,
            transcendentals=0,
            bytes_accessed=4 * (rows * width + frames * width + 2 * rows * frames),
        ),
    )(*operands)
    return result if norms else result[0]


def _update_kernel(offset_ref, start_ref, weighted_ref, image_ref, matrix_ref, *rest):
    out_ref = rest[-1]
    frames = image_ref.shape[0]
    weighted_hi, weighted_lo = _split(weighted_ref[...])
    both = jnp.concatenate([weighted_hi, weighted_lo], axis=0)
    matrix_hi, matrix_lo = _split(matrix_ref[...])
    paired = jnp.dot(both, matrix_hi, preferred_element_type=jnp.float32)
    cross = jnp.dot(weighted_hi, matrix_lo, preferred_element_type=jnp.float32)
    out_ref[...] = jnp.maximum(
        image_ref[...] + (paired[:frames] + paired[frames:] + cross), 0.0
    )


def update(weighted, image, system, block, rows, first, width, after=None):
    frames = image.shape[0]
    tile = min(TILE, width // 2)
    chunked = image.shape[1] != width
    start = np.array([first // tile], np.int32)
    extra_specs, extra = [], []
    if after is not None:
        block_shape = (8, min(128, after.shape[1]))
        extra_specs, extra = [pl.BlockSpec(block_shape, lambda j, off, st: (0, 0))], [after]
    return pl.pallas_call(
        _update_kernel,
        out_shape=jax.ShapeDtypeStruct((frames, width), jnp.float32),
        grid_spec=pltpu.PrefetchScalarGridSpec(
            num_scalar_prefetch=2,
            grid=(width // tile,),
            in_specs=[
                pl.BlockSpec((frames, rows), lambda j, off, st: (0, 0)),
                pl.BlockSpec((frames, tile), lambda j, off, st: (0, st[0] * chunked + j)),
                pl.BlockSpec((rows, tile), lambda j, off, st: (off[0], st[0] + j)),
            ]
            + extra_specs,
            out_specs=pl.BlockSpec((frames, tile), lambda j, off, st: (0, j)),
        ),
        compiler_params=pltpu.CompilerParams(
            dimension_semantics=("arbitrary",), vmem_limit_bytes=48 * 1024 * 1024
        ),
        cost_estimate=pl.CostEstimate(
            flops=2 * rows * width * frames * 3,
            transcendentals=0,
            bytes_accessed=4 * (rows * width + 2 * frames * width + rows * frames),
        ),
    )(block, start, weighted, image, system, *extra)


def _middle_kernel(with_norms, order_ref, weighted_ref, image_ref, first_ref, second_ref, *rest):
    image_out, total_ref = rest[0], rest[1]
    frames = image_ref.shape[0]

    @pl.when(pl.program_id(0) == 0)
    def _():
        total_ref[...] = jnp.zeros_like(total_ref)
        if with_norms:
            rest[2][...] = jnp.zeros_like(rest[2])

    weighted_hi, weighted_lo = _split(weighted_ref[...])
    both = jnp.concatenate([weighted_hi, weighted_lo], axis=0)
    first_hi, first_lo = _split(first_ref[...])
    paired = jnp.dot(both, first_hi, preferred_element_type=jnp.float32)
    cross = jnp.dot(weighted_hi, first_lo, preferred_element_type=jnp.float32)
    fresh = jnp.maximum(image_ref[...] + (paired[:frames] + paired[frames:] + cross), 0.0)
    image_out[...] = fresh

    fresh_hi, fresh_lo = _split(fresh)
    stacked = jnp.concatenate([fresh_hi, fresh_lo], axis=0)
    second = second_ref[...]
    second_hi, second_lo = _split(second)
    paired = lax.dot_general(second_hi, stacked, _DN, preferred_element_type=jnp.float32)
    cross = lax.dot_general(second_lo, fresh_hi, _DN, preferred_element_type=jnp.float32)
    total_ref[...] += paired[:, :frames] + paired[:, frames:] + cross
    if with_norms:
        rest[2][...] += jnp.sum(second * second, axis=1, keepdims=True)


def middle(weighted, image, system, sequence, rows, norms):
    frames, voxels = image.shape
    tile = MIDDLE_TILE
    out_shape = [
        jax.ShapeDtypeStruct((frames, voxels), jnp.float32),
        jax.ShapeDtypeStruct((rows, frames), jnp.float32),
    ]
    out_specs = [
        pl.BlockSpec((frames, tile), lambda j, off: (0, j)),
        pl.BlockSpec((rows, frames), lambda j, off: (0, 0)),
    ]
    if norms:
        out_shape.append(jax.ShapeDtypeStruct((rows, 1), jnp.float32))
        out_specs.append(pl.BlockSpec((rows, 1), lambda j, off: (0, 0)))
    return pl.pallas_call(
        functools.partial(_middle_kernel, norms),
        out_shape=out_shape,
        grid_spec=pltpu.PrefetchScalarGridSpec(
            num_scalar_prefetch=1,
            grid=(voxels // tile,),
            in_specs=[
                pl.BlockSpec((frames, rows), lambda j, off: (0, 0)),
                pl.BlockSpec((frames, tile), lambda j, off: (0, j)),
                pl.BlockSpec((rows, tile), lambda j, off: (off[0], j)),
                pl.BlockSpec((rows, tile), lambda j, off: (off[1], j)),
            ],
            out_specs=out_specs,
        ),
        compiler_params=pltpu.CompilerParams(
            dimension_semantics=("arbitrary",), vmem_limit_bytes=56 * 1024 * 1024
        ),
        cost_estimate=pl.CostEstimate(
            flops=4 * rows * voxels * frames * 3,
            transcendentals=0,
            bytes_accessed=4 * (2 * rows * voxels + 2 * frames * voxels + 2 * rows * frames),
        ),
    )(sequence, weighted, image, system, system)


def local(system, measured, row_class, band_weight, order):
    cycle_size = lax.axis_size("row")
    position = lax.axis_index("row")
    rows_here = system.shape[0]
    voxels = system.shape[1]
    subblocks = order.shape[1]
    subblock_rows = rows_here // subblocks
    band_hits = (
        row_class[:, None] == jnp.arange(band_weight.shape[0], dtype=jnp.int32)[None, :]
    ).astype(jnp.float32)
    band = jnp.dot(band_hits, band_weight, precision=lax.Precision.HIGHEST)
    sequence = order[0]
    ordered = []
    for which in range(subblocks):
        first_row = sequence[which] * subblock_rows
        ordered.append(
            (
                sequence[which:which + 1],
                lax.dynamic_slice_in_dim(band, first_row, subblock_rows, 0),
                first_row,
            )
        )
    first_rows = lax.dynamic_slice_in_dim(system, ordered[0][2], subblock_rows, 0)
    weight0 = ordered[0][1] / (jnp.sum(first_rows * first_rows, axis=1) + epsilon)
    width = voxels // CHUNKS
    chunks = [jnp.zeros((BATCH_FRAMES, width), jnp.float32) for _ in range(CHUNKS)]
    head = None
    for visit_no in range(STEPS):
        owner = (position - visit_no) % cycle_size
        first_frame = owner * BATCH_FRAMES
        (block0, _, row0), (block1, band1, row1) = ordered
        signal0 = lax.dynamic_slice(measured, (row0, first_frame), (subblock_rows, BATCH_FRAMES))
        signal1 = lax.dynamic_slice(measured, (row1, first_frame), (subblock_rows, BATCH_FRAMES))
        if visit_no == 0:
            residual = signal0.T
        else:
            total = head
            for index in range(1, CHUNKS):
                total = forward_t(chunks[index], system, block0, subblock_rows, total, index * width)
            residual = (signal0 - total).T
        image = jnp.concatenate(chunks, axis=1)
        image, total, *norms = middle(
            residual * weight0[None, :], image, system, sequence, subblock_rows, visit_no == 0
        )
        if visit_no == 0:
            weight1 = band1 / (norms[0][:, 0] + epsilon)
        weighted = (signal1 - total).T * weight1[None, :]
        last = visit_no + 1 == STEPS
        steps = 1 if not last else 1 - STEPS
        chunks = []
        for index in range(CHUNKS):
            after = None
            if last and index >= 2:
                after = chunks[index - 2]
            elif not last and index == CHUNKS - 1:
                head = forward_t(chunks[0], system, block0, subblock_rows, None, 0)
                after = head
            piece = update(
                weighted, image, system, block1, subblock_rows, index * width, width, after
            )
            chunks.append(shifted(piece, "row", steps))
    return jnp.concatenate(chunks, axis=1)


def solution(mesh):
    return jax.shard_map(
        local,
        mesh=mesh,
        in_specs=(
            P(("grp", "row"), None),
            P(("grp", "row"), None),
            P(("grp", "row")),
            P("grp"),
            P(("grp", "row"), None),
        ),
        out_specs=P(("grp", "row"), None),
        check_vma=False,
    )
```

```python
import functools

import jax
import numpy as np
import jax.numpy as jnp
from jax import lax
from jax.experimental import pallas as pl
from jax.experimental.pallas import tpu as pltpu
from jax.sharding import PartitionSpec as P

BATCH_FRAMES = 32
STEPS = 6
CHUNKS = 4


epsilon = 1e-06


def shifted(value, axis, steps):
    count = lax.axis_size(axis)
    pairs = [(source, (source + steps) % count) for source in range(count)]
    return lax.ppermute(value, axis, pairs)


TILE = 4096
_DN = (((1,), (1,)), ((), ()))
_TN = (((0,), (0,)), ((), ()))


def _split(value):
    high = value.astype(jnp.bfloat16)
    return high, (value - high.astype(jnp.float32)).astype(jnp.bfloat16)


def _forward_kernel(with_total, with_norms, offset_ref, start_ref, image_ref, matrix_ref, *rest):
    out_ref = rest[1] if with_total else rest[0]
    norm_ref = rest[-1] if with_norms else None

    @pl.when(pl.program_id(0) == 0)
    def _():
        if with_total:
            out_ref[...] = rest[0][...]
        else:
            out_ref[...] = jnp.zeros_like(out_ref)
        if with_norms:
            norm_ref[...] = jnp.zeros_like(norm_ref)

    if with_norms:
        square = matrix_ref[...] * matrix_ref[...]
        norm_ref[...] += jnp.sum(square, axis=1, keepdims=True)

    frames = image_ref.shape[0]
    image_hi, image_lo = _split(image_ref[...])
    both = jnp.concatenate([image_hi, image_lo], axis=0)
    matrix_hi, matrix_lo = _split(matrix_ref[...])
    paired = lax.dot_general(matrix_hi, both, _DN, preferred_element_type=jnp.float32)
    cross = lax.dot_general(matrix_lo, image_hi, _DN, preferred_element_type=jnp.float32)
    out_ref[...] += paired[:, :frames] + paired[:, frames:] + cross


def forward_t(image, system, block, rows, total, first, norms=False):
    frames, width = image.shape
    tile = min(TILE, width // 2)
    start = np.array([first // tile], np.int32)
    operands, specs, aliases = [block, start, image, system], [], {}
    if total is not None:
        operands.append(total)
        specs = [pl.BlockSpec((rows, frames), lambda j, off, st: (0, 0))]
        aliases = {4: 0}
    out_shape = [jax.ShapeDtypeStruct((rows, frames), jnp.float32)]
    out_specs = [pl.BlockSpec((rows, frames), lambda j, off, st: (0, 0))]
    if norms:
        out_shape.append(jax.ShapeDtypeStruct((rows, 1), jnp.float32))
        out_specs.append(pl.BlockSpec((rows, 1), lambda j, off, st: (0, 0)))
    result = pl.pallas_call(
        functools.partial(_forward_kernel, total is not None, norms),
        out_shape=out_shape,
        grid_spec=pltpu.PrefetchScalarGridSpec(
            num_scalar_prefetch=2,
            grid=(width // tile,),
            in_specs=[
                pl.BlockSpec((frames, tile), lambda j, off, st: (0, j)),
                pl.BlockSpec((rows, tile), lambda j, off, st: (off[0], st[0] + j)),
            ]
            + specs,
            out_specs=out_specs,
        ),
        input_output_aliases=aliases,
        compiler_params=pltpu.CompilerParams(
            dimension_semantics=("arbitrary",), vmem_limit_bytes=48 * 1024 * 1024
        ),
        cost_estimate=pl.CostEstimate(
            flops=2 * rows * width * frames * 3,
            transcendentals=0,
            bytes_accessed=4 * (rows * width + frames * width + 2 * rows * frames),
        ),
    )(*operands)
    return result if norms else result[0]


def _update_kernel(offset_ref, start_ref, weighted_ref, image_ref, matrix_ref, *rest):
    out_ref = rest[-1]
    frames = image_ref.shape[0]
    weighted_hi, weighted_lo = _split(weighted_ref[...])
    both = jnp.concatenate([weighted_hi, weighted_lo], axis=1)
    matrix_hi, matrix_lo = _split(matrix_ref[...])
    paired = lax.dot_general(both, matrix_hi, _TN, preferred_element_type=jnp.float32)
    cross = lax.dot_general(weighted_hi, matrix_lo, _TN, preferred_element_type=jnp.float32)
    out_ref[...] = jnp.maximum(
        image_ref[...] + (paired[:frames] + paired[frames:] + cross), 0.0
    )


def update(weighted, image, system, block, rows, first, width, after=None):
    frames = image.shape[0]
    tile = min(TILE, width // 2)
    chunked = image.shape[1] != width
    start = np.array([first // tile], np.int32)
    extra_specs, extra = [], []
    if after is not None:
        block_shape = (8, min(128, after.shape[1]))
        extra_specs, extra = [pl.BlockSpec(block_shape, lambda j, off, st: (0, 0))], [after]
    return pl.pallas_call(
        _update_kernel,
        out_shape=jax.ShapeDtypeStruct((frames, width), jnp.float32),
        grid_spec=pltpu.PrefetchScalarGridSpec(
            num_scalar_prefetch=2,
            grid=(width // tile,),
            in_specs=[
                pl.BlockSpec((rows, frames), lambda j, off, st: (0, 0)),
                pl.BlockSpec((frames, tile), lambda j, off, st: (0, st[0] * chunked + j)),
                pl.BlockSpec((rows, tile), lambda j, off, st: (off[0], st[0] + j)),
            ]
            + extra_specs,
            out_specs=pl.BlockSpec((frames, tile), lambda j, off, st: (0, j)),
        ),
        compiler_params=pltpu.CompilerParams(
            dimension_semantics=("arbitrary",), vmem_limit_bytes=48 * 1024 * 1024
        ),
        cost_estimate=pl.CostEstimate(
            flops=2 * rows * width * frames * 3,
            transcendentals=0,
            bytes_accessed=4 * (rows * width + 2 * frames * width + rows * frames),
        ),
    )(block, start, weighted, image, system, *extra)


def local(system, measured, row_class, band_weight, order):
    cycle_size = lax.axis_size("row")
    position = lax.axis_index("row")
    rows_here = system.shape[0]
    voxels = system.shape[1]
    subblocks = order.shape[1]
    subblock_rows = rows_here // subblocks
    band_hits = (
        row_class[:, None] == jnp.arange(band_weight.shape[0], dtype=jnp.int32)[None, :]
    ).astype(jnp.float32)
    band = jnp.dot(band_hits, band_weight, precision=lax.Precision.HIGHEST)
    sequence = order[0]
    ordered = []
    for which in range(subblocks):
        first_row = sequence[which] * subblock_rows
        ordered.append(
            (
                sequence[which:which + 1],
                lax.dynamic_slice_in_dim(band, first_row, subblock_rows, 0),
                first_row,
            )
        )
    first_rows = lax.dynamic_slice_in_dim(system, ordered[0][2], subblock_rows, 0)
    weight0 = ordered[0][1] / (jnp.sum(first_rows * first_rows, axis=1) + epsilon)
    width = voxels // CHUNKS
    chunks = [jnp.zeros((BATCH_FRAMES, width), jnp.float32) for _ in range(CHUNKS)]
    head = None
    for visit_no in range(STEPS):
        owner = (position - visit_no) % cycle_size
        first_frame = owner * BATCH_FRAMES
        (block0, _, row0), (block1, band1, row1) = ordered
        signal0 = lax.dynamic_slice(measured, (row0, first_frame), (subblock_rows, BATCH_FRAMES))
        signal1 = lax.dynamic_slice(measured, (row1, first_frame), (subblock_rows, BATCH_FRAMES))
        if visit_no == 0:
            residual = signal0
        else:
            total = head
            for index in range(1, CHUNKS):
                total = forward_t(chunks[index], system, block0, subblock_rows, total, index * width)
            residual = signal0 - total
        image = jnp.concatenate(chunks, axis=1)
        image = update(residual * weight0[:, None], image, system, block0, subblock_rows, 0, voxels)
        if visit_no == 0:
            total, norms = forward_t(image, system, block1, subblock_rows, None, 0, True)
            weight1 = band1 / (norms[:, 0] + epsilon)
        else:
            total = forward_t(image, system, block1, subblock_rows, None, 0)
        weighted = (signal1 - total) * weight1[:, None]
        last = visit_no + 1 == STEPS
        steps = 1 if not last else 1 - STEPS
        chunks = []
        for index in range(CHUNKS):
            after = None
            if last and index >= 2:
                after = chunks[index - 2]
            elif not last and index == CHUNKS - 1:
                head = forward_t(chunks[0], system, block0, subblock_rows, None, 0)
                after = head
            piece = update(
                weighted, image, system, block1, subblock_rows, index * width, width, after
            )
            chunks.append(shifted(piece, "row", steps))
    return jnp.concatenate(chunks, axis=1)


def solution(mesh):
    return jax.shard_map(
        local,
        mesh=mesh,
        in_specs=(
            P(("grp", "row"), None),
            P(("grp", "row"), None),
            P(("grp", "row")),
            P("grp"),
            P(("grp", "row"), None),
        ),
        out_specs=P(("grp", "row"), None),
        check_vma=False,
    )
```

```python
import functools

import jax
import numpy as np
import jax.numpy as jnp
from jax import lax
from jax.experimental import pallas as pl
from jax.experimental.pallas import tpu as pltpu
from jax.sharding import PartitionSpec as P

BATCH_FRAMES = 32
STEPS = 6
CHUNKS = 4


epsilon = 1e-06


def shifted(value, axis, steps):
    count = lax.axis_size(axis)
    pairs = [(source, (source + steps) % count) for source in range(count)]
    return lax.ppermute(value, axis, pairs)


TILE = 4096
_DN = (((1,), (1,)), ((), ()))
_TN = (((0,), (0,)), ((), ()))


def _split(value):
    high = value.astype(jnp.bfloat16)
    return high, (value - high.astype(jnp.float32)).astype(jnp.bfloat16)


def _forward_kernel(with_total, with_norms, offset_ref, start_ref, image_ref, matrix_ref, *rest):
    out_ref = rest[1] if with_total else rest[0]
    norm_ref = rest[-1] if with_norms else None

    @pl.when(pl.program_id(0) == 0)
    def _():
        if with_total:
            out_ref[...] = rest[0][...]
        else:
            out_ref[...] = jnp.zeros_like(out_ref)
        if with_norms:
            norm_ref[...] = jnp.zeros_like(norm_ref)

    if with_norms:
        square = matrix_ref[...] * matrix_ref[...]
        norm_ref[...] += jnp.sum(square, axis=1, keepdims=True)

    frames = image_ref.shape[0]
    image_hi, image_lo = _split(image_ref[...])
    both = jnp.concatenate([image_hi, image_lo], axis=0)
    matrix_hi, matrix_lo = _split(matrix_ref[...])
    paired = lax.dot_general(matrix_hi, both, _DN, preferred_element_type=jnp.float32)
    cross = lax.dot_general(matrix_lo, image_hi, _DN, preferred_element_type=jnp.float32)
    out_ref[...] += paired[:, :frames] + paired[:, frames:] + cross


def forward_t(image, system, block, rows, total, first, norms=False):
    frames, width = image.shape
    tile = min(TILE, width // 2)
    start = np.array([first // tile], np.int32)
    operands, specs, aliases = [block, start, image, system], [], {}
    if total is not None:
        operands.append(total)
        specs = [pl.BlockSpec((rows, frames), lambda j, off, st: (0, 0))]
        aliases = {4: 0}
    out_shape = [jax.ShapeDtypeStruct((rows, frames), jnp.float32)]
    out_specs = [pl.BlockSpec((rows, frames), lambda j, off, st: (0, 0))]
    if norms:
        out_shape.append(jax.ShapeDtypeStruct((rows, 1), jnp.float32))
        out_specs.append(pl.BlockSpec((rows, 1), lambda j, off, st: (0, 0)))
    result = pl.pallas_call(
        functools.partial(_forward_kernel, total is not None, norms),
        out_shape=out_shape,
        grid_spec=pltpu.PrefetchScalarGridSpec(
            num_scalar_prefetch=2,
            grid=(width // tile,),
            in_specs=[
                pl.BlockSpec((frames, tile), lambda j, off, st: (0, j)),
                pl.BlockSpec((rows, tile), lambda j, off, st: (off[0], st[0] + j)),
            ]
            + specs,
            out_specs=out_specs,
        ),
        input_output_aliases=aliases,
        compiler_params=pltpu.CompilerParams(
            dimension_semantics=("arbitrary",), vmem_limit_bytes=48 * 1024 * 1024
        ),
        cost_estimate=pl.CostEstimate(
            flops=2 * rows * width * frames * 3,
            transcendentals=0,
            bytes_accessed=4 * (rows * width + frames * width + 2 * rows * frames),
        ),
    )(*operands)
    return result if norms else result[0]


def _update_kernel(with_total, offset_ref, start_ref, owners_ref, signal_ref, *rest):
    total_ref = rest[0] if with_total else None
    weight_ref, image_ref, matrix_ref = rest[with_total:with_total + 3]
    out_ref = rest[-1]
    frames = image_ref.shape[0]
    residual = signal_ref[...]
    if with_total:
        residual = residual - total_ref[...]
    weighted = residual * weight_ref[...]
    weighted_hi, weighted_lo = _split(weighted)
    both = jnp.concatenate([weighted_hi, weighted_lo], axis=1)
    matrix_hi, matrix_lo = _split(matrix_ref[...])
    paired = lax.dot_general(both, matrix_hi, _TN, preferred_element_type=jnp.float32)
    cross = lax.dot_general(weighted_hi, matrix_lo, _TN, preferred_element_type=jnp.float32)
    out_ref[...] = jnp.maximum(
        image_ref[...] + (paired[:frames] + paired[frames:] + cross), 0.0
    )


def update(signals, owners, visit, total, weight, image, system, block, rows, first, width,
           after=None):
    frames = image.shape[0]
    tile = min(TILE, width // 2)
    chunked = image.shape[1] != width
    start = np.array([first // tile, visit], np.int32)
    specs = [pl.BlockSpec((None, rows, frames), lambda j, off, st, own: (own[st[1]], off[0], 0))]
    operands = [signals]
    if total is not None:
        specs.append(pl.BlockSpec((rows, frames), lambda j, off, st, own: (0, 0)))
        operands.append(total)
    specs += [
        pl.BlockSpec((rows, 1), lambda j, off, st, own: (0, 0)),
        pl.BlockSpec((frames, tile), lambda j, off, st, own: (0, st[0] * chunked + j)),
        pl.BlockSpec((rows, tile), lambda j, off, st, own: (off[0], st[0] + j)),
    ]
    operands += [weight, image, system]
    if after is not None:
        block_shape = (8, min(128, after.shape[1]))
        specs.append(pl.BlockSpec(block_shape, lambda j, off, st, own: (0, 0)))
        operands.append(after)
    return pl.pallas_call(
        functools.partial(_update_kernel, total is not None),
        out_shape=jax.ShapeDtypeStruct((frames, width), jnp.float32),
        grid_spec=pltpu.PrefetchScalarGridSpec(
            num_scalar_prefetch=3,
            grid=(width // tile,),
            in_specs=specs,
            out_specs=pl.BlockSpec((frames, tile), lambda j, off, st, own: (0, j)),
        ),
        compiler_params=pltpu.CompilerParams(
            dimension_semantics=("arbitrary",), vmem_limit_bytes=48 * 1024 * 1024
        ),
        cost_estimate=pl.CostEstimate(
            flops=2 * rows * width * frames * 3,
            transcendentals=0,
            bytes_accessed=4 * (rows * width + 2 * frames * width + rows * frames),
        ),
    )(block, start, owners, *operands)


def local(system, measured, row_class, band_weight, order):
    cycle_size = lax.axis_size("row")
    position = lax.axis_index("row")
    rows_here = system.shape[0]
    voxels = system.shape[1]
    subblocks = order.shape[1]
    subblock_rows = rows_here // subblocks
    band_hits = (
        row_class[:, None] == jnp.arange(band_weight.shape[0], dtype=jnp.int32)[None, :]
    ).astype(jnp.float32)
    band = jnp.dot(band_hits, band_weight, precision=lax.Precision.HIGHEST)
    sequence = order[0]
    ordered = []
    for which in range(subblocks):
        first_row = sequence[which] * subblock_rows
        ordered.append(
            (
                sequence[which:which + 1],
                lax.dynamic_slice_in_dim(band, first_row, subblock_rows, 0),
                first_row,
            )
        )
    first_rows = lax.dynamic_slice_in_dim(system, ordered[0][2], subblock_rows, 0)
    weight0 = (ordered[0][1] / (jnp.sum(first_rows * first_rows, axis=1) + epsilon))[:, None]
    batches = measured.shape[1] // BATCH_FRAMES
    signals = measured.reshape(rows_here, batches, BATCH_FRAMES).transpose(1, 0, 2)
    owners = (position - jnp.arange(STEPS, dtype=jnp.int32)) % cycle_size
    width = voxels // CHUNKS
    chunks = [jnp.zeros((BATCH_FRAMES, width), jnp.float32) for _ in range(CHUNKS)]
    head = None
    for visit_no in range(STEPS):
        owner = (position - visit_no) % cycle_size
        first_frame = owner * BATCH_FRAMES
        (block0, _, row0), (block1, band1, row1) = ordered
        total = None
        if visit_no > 0:
            total = head
            for index in range(1, CHUNKS):
                total = forward_t(chunks[index], system, block0, subblock_rows, total, index * width)
        image = jnp.concatenate(chunks, axis=1)
        image = update(
            signals, owners, visit_no, total, weight0, image, system, block0, subblock_rows, 0, voxels
        )
        if visit_no == 0:
            total, norms = forward_t(image, system, block1, subblock_rows, None, 0, True)
            weight1 = (band1 / (norms[:, 0] + epsilon))[:, None]
        else:
            total = forward_t(image, system, block1, subblock_rows, None, 0)
        last = visit_no + 1 == STEPS
        steps = 1 if not last else 1 - STEPS
        chunks = []
        for index in range(CHUNKS):
            after = None
            if last and index >= 2:
                after = chunks[index - 2]
            elif not last and index == CHUNKS - 1:
                head = forward_t(chunks[0], system, block0, subblock_rows, None, 0)
                after = head
            piece = update(
                signals, owners, visit_no, total, weight1, image, system, block1,
                subblock_rows, index * width, width, after,
            )
            chunks.append(shifted(piece, "row", steps))
    return jnp.concatenate(chunks, axis=1)


def solution(mesh):
    return jax.shard_map(
        local,
        mesh=mesh,
        in_specs=(
            P(("grp", "row"), None),
            P(("grp", "row"), None),
            P(("grp", "row")),
            P("grp"),
            P(("grp", "row"), None),
        ),
        out_specs=P(("grp", "row"), None),
        check_vma=False,
    )
```

```python
import functools

import jax
import numpy as np
import jax.numpy as jnp
from jax import lax
from jax.experimental import pallas as pl
from jax.experimental.pallas import tpu as pltpu
from jax.sharding import PartitionSpec as P

BATCH_FRAMES = 32
STEPS = 6
CHUNKS = 4


epsilon = 1e-06


def shifted(value, axis, steps):
    count = lax.axis_size(axis)
    pairs = [(source, (source + steps) % count) for source in range(count)]
    return lax.ppermute(value, axis, pairs)


TILE = 4096
_DN = (((1,), (1,)), ((), ()))
_TN = (((0,), (0,)), ((), ()))


def _split(value):
    high = value.astype(jnp.bfloat16)
    return high, (value - high.astype(jnp.float32)).astype(jnp.bfloat16)


def _forward_kernel(with_total, with_norms, offset_ref, start_ref, image_ref, matrix_ref, *rest):
    out_ref = rest[1] if with_total else rest[0]
    norm_ref = rest[-1] if with_norms else None

    @pl.when(pl.program_id(0) == 0)
    def _():
        if with_total:
            out_ref[...] = rest[0][...]
        else:
            out_ref[...] = jnp.zeros_like(out_ref)
        if with_norms:
            norm_ref[...] = jnp.zeros_like(norm_ref)

    if with_norms:
        square = matrix_ref[...] * matrix_ref[...]
        norm_ref[...] += jnp.sum(square, axis=1, keepdims=True)

    frames = image_ref.shape[0]
    image_hi, image_lo = _split(image_ref[...])
    both = jnp.concatenate([image_hi, image_lo], axis=0)
    matrix_hi, matrix_lo = _split(matrix_ref[...])
    paired = lax.dot_general(matrix_hi, both, _DN, preferred_element_type=jnp.float32)
    cross = lax.dot_general(matrix_lo, image_hi, _DN, preferred_element_type=jnp.float32)
    out_ref[...] += paired[:, :frames] + paired[:, frames:] + cross


def forward_t(image, system, block, rows, total, first, norms=False):
    frames, width = image.shape
    tile = min(TILE, width // 2)
    start = np.array([first // tile], np.int32)
    operands, specs, aliases = [block, start, image, system], [], {}
    if total is not None:
        operands.append(total)
        specs = [pl.BlockSpec((rows, frames), lambda j, off, st: (0, 0))]
        aliases = {4: 0}
    out_shape = [jax.ShapeDtypeStruct((rows, frames), jnp.float32)]
    out_specs = [pl.BlockSpec((rows, frames), lambda j, off, st: (0, 0))]
    if norms:
        out_shape.append(jax.ShapeDtypeStruct((rows, 1), jnp.float32))
        out_specs.append(pl.BlockSpec((rows, 1), lambda j, off, st: (0, 0)))
    result = pl.pallas_call(
        functools.partial(_forward_kernel, total is not None, norms),
        out_shape=out_shape,
        grid_spec=pltpu.PrefetchScalarGridSpec(
            num_scalar_prefetch=2,
            grid=(width // tile,),
            in_specs=[
                pl.BlockSpec((frames, tile), lambda j, off, st: (0, j)),
                pl.BlockSpec((rows, tile), lambda j, off, st: (off[0], st[0] + j)),
            ]
            + specs,
            out_specs=out_specs,
        ),
        input_output_aliases=aliases,
        compiler_params=pltpu.CompilerParams(
            dimension_semantics=("arbitrary",), vmem_limit_bytes=48 * 1024 * 1024
        ),
        cost_estimate=pl.CostEstimate(
            flops=2 * rows * width * frames * 3,
            transcendentals=0,
            bytes_accessed=4 * (rows * width + frames * width + 2 * rows * frames),
        ),
    )(*operands)
    return result if norms else result[0]


def _update_kernel(offset_ref, start_ref, weighted_ref, image_ref, matrix_ref, *rest):
    out_ref = rest[-1]
    frames = image_ref.shape[0]
    weighted_hi, weighted_lo = _split(weighted_ref[...])
    both = jnp.concatenate([weighted_hi, weighted_lo], axis=1)
    matrix_hi, matrix_lo = _split(matrix_ref[...])
    paired = lax.dot_general(both, matrix_hi, _TN, preferred_element_type=jnp.float32)
    cross = lax.dot_general(weighted_hi, matrix_lo, _TN, preferred_element_type=jnp.float32)
    out_ref[...] = jnp.maximum(
        image_ref[...] + (paired[:frames] + paired[frames:] + cross), 0.0
    )


def update(weighted, image, system, block, rows, first, width, after=None):
    frames = image.shape[0]
    tile = min(TILE, width // 2)
    chunked = image.shape[1] != width
    start = np.array([first // tile], np.int32)
    extra_specs, extra = [], []
    if after is not None:
        block_shape = (8, min(128, after.shape[1]))
        extra_specs, extra = [pl.BlockSpec(block_shape, lambda j, off, st: (0, 0))], [after]
    return pl.pallas_call(
        _update_kernel,
        out_shape=jax.ShapeDtypeStruct((frames, width), jnp.float32),
        grid_spec=pltpu.PrefetchScalarGridSpec(
            num_scalar_prefetch=2,
            grid=(width // tile,),
            in_specs=[
                pl.BlockSpec((rows, frames), lambda j, off, st: (0, 0)),
                pl.BlockSpec((frames, tile), lambda j, off, st: (0, st[0] * chunked + j)),
                pl.BlockSpec((rows, tile), lambda j, off, st: (off[0], st[0] + j)),
            ]
            + extra_specs,
            out_specs=pl.BlockSpec((frames, tile), lambda j, off, st: (0, j)),
        ),
        compiler_params=pltpu.CompilerParams(
            dimension_semantics=("arbitrary",), vmem_limit_bytes=48 * 1024 * 1024
        ),
        cost_estimate=pl.CostEstimate(
            flops=2 * rows * width * frames * 3,
            transcendentals=0,
            bytes_accessed=4 * (rows * width + 2 * frames * width + rows * frames),
        ),
    )(block, start, weighted, image, system, *extra)


def local(system, measured, row_class, band_weight, order):
    cycle_size = lax.axis_size("row")
    position = lax.axis_index("row")
    rows_here = system.shape[0]
    voxels = system.shape[1]
    subblocks = order.shape[1]
    subblock_rows = rows_here // subblocks
    band_hits = (
        row_class[:, None] == jnp.arange(band_weight.shape[0], dtype=jnp.int32)[None, :]
    ).astype(jnp.float32)
    band = jnp.dot(band_hits, band_weight, precision=lax.Precision.HIGHEST)
    sequence = order[0]
    ordered = []
    for which in range(subblocks):
        first_row = sequence[which] * subblock_rows
        ordered.append(
            (
                sequence[which:which + 1],
                lax.dynamic_slice_in_dim(band, first_row, subblock_rows, 0),
                first_row,
            )
        )
    first_rows = lax.dynamic_slice_in_dim(system, ordered[0][2], subblock_rows, 0)
    weight0 = ordered[0][1] / (jnp.sum(first_rows * first_rows, axis=1) + epsilon)
    width = voxels // CHUNKS
    chunks = [jnp.zeros((BATCH_FRAMES, width), jnp.float32) for _ in range(CHUNKS)]
    head = None
    for visit_no in range(STEPS):
        owner = (position - visit_no) % cycle_size
        first_frame = owner * BATCH_FRAMES
        (block0, _, row0), (block1, band1, row1) = ordered
        signal0 = lax.dynamic_slice(measured, (row0, first_frame), (subblock_rows, BATCH_FRAMES))
        signal1 = lax.dynamic_slice(measured, (row1, first_frame), (subblock_rows, BATCH_FRAMES))
        if visit_no == 0:
            residual = signal0
        else:
            total = head
            for index in range(1, CHUNKS):
                total = forward_t(chunks[index], system, block0, subblock_rows, total, index * width)
            residual = signal0 - total
        image = jnp.concatenate(chunks, axis=1)
        image = update(residual * weight0[:, None], image, system, block0, subblock_rows, 0, voxels)
        if visit_no == 0:
            total, norms = forward_t(image, system, block1, subblock_rows, None, 0, True)
            weight1 = band1 / (norms[:, 0] + epsilon)
        else:
            total = forward_t(image, system, block1, subblock_rows, None, 0)
        weighted = (signal1 - total) * weight1[:, None]
        last = visit_no + 1 == STEPS
        steps = 1 if not last else 1 - STEPS
        chunks = []
        for index in range(CHUNKS):
            after = None
            if not last and index == CHUNKS - 1:
                head = forward_t(chunks[0], system, block0, subblock_rows, None, 0)
                after = head
            piece = update(
                weighted, image, system, block1, subblock_rows, index * width, width, after
            )
            chunks.append(shifted(piece, "row", steps))
    return jnp.concatenate(chunks, axis=1)


def solution(mesh):
    return jax.shard_map(
        local,
        mesh=mesh,
        in_specs=(
            P(("grp", "row"), None),
            P(("grp", "row"), None),
            P(("grp", "row")),
            P("grp"),
            P(("grp", "row"), None),
        ),
        out_specs=P(("grp", "row"), None),
        check_vma=False,
    )
```

```python
import functools

import jax
import numpy as np
import jax.numpy as jnp
from jax import lax
from jax.experimental import pallas as pl
from jax.experimental.pallas import tpu as pltpu
from jax.sharding import PartitionSpec as P

BATCH_FRAMES = 32
STEPS = 6
CHUNKS = 4


epsilon = 1e-06


def shifted(value, axis, steps):
    count = lax.axis_size(axis)
    pairs = [(source, (source + steps) % count) for source in range(count)]
    return lax.ppermute(value, axis, pairs)


TILE = 4096
SUB = 512
_DN = (((1,), (1,)), ((), ()))
_TN = (((0,), (0,)), ((), ()))


def _split(value):
    high = value.astype(jnp.bfloat16)
    return high, (value - high.astype(jnp.float32)).astype(jnp.bfloat16)


def _forward_kernel(with_total, with_norms, offset_ref, start_ref, image_ref, matrix_ref, *rest):
    out_ref = rest[1] if with_total else rest[0]
    norm_ref = rest[-1] if with_norms else None

    @pl.when(pl.program_id(0) == 0)
    def _():
        if with_total:
            out_ref[...] = rest[0][...]
        else:
            out_ref[...] = jnp.zeros_like(out_ref)
        if with_norms:
            norm_ref[...] = jnp.zeros_like(norm_ref)

    if with_norms:
        square = matrix_ref[...] * matrix_ref[...]
        norm_ref[...] += jnp.sum(square, axis=1, keepdims=True)

    frames = image_ref.shape[0]

    def part(index, total):
        cols = pl.ds(pl.multiple_of(index * SUB, SUB), SUB)
        image_hi, image_lo = _split(image_ref[:, cols])
        both = jnp.concatenate([image_hi, image_lo], axis=0)
        matrix_hi, matrix_lo = _split(matrix_ref[:, cols])
        paired = lax.dot_general(matrix_hi, both, _DN, preferred_element_type=jnp.float32)
        cross = lax.dot_general(matrix_lo, image_hi, _DN, preferred_element_type=jnp.float32)
        return total + (paired[:, :frames] + paired[:, frames:] + cross)

    out_ref[...] += lax.fori_loop(
        0, image_ref.shape[1] // SUB, part, jnp.zeros(out_ref.shape, jnp.float32)
    )


def forward_t(image, system, block, rows, total, first, norms=False):
    frames, width = image.shape
    tile = min(TILE, width // 2)
    start = np.array([first // tile], np.int32)
    operands, specs, aliases = [block, start, image, system], [], {}
    if total is not None:
        operands.append(total)
        specs = [pl.BlockSpec((rows, frames), lambda j, off, st: (0, 0))]
        aliases = {4: 0}
    out_shape = [jax.ShapeDtypeStruct((rows, frames), jnp.float32)]
    out_specs = [pl.BlockSpec((rows, frames), lambda j, off, st: (0, 0))]
    if norms:
        out_shape.append(jax.ShapeDtypeStruct((rows, 1), jnp.float32))
        out_specs.append(pl.BlockSpec((rows, 1), lambda j, off, st: (0, 0)))
    result = pl.pallas_call(
        functools.partial(_forward_kernel, total is not None, norms),
        out_shape=out_shape,
        grid_spec=pltpu.PrefetchScalarGridSpec(
            num_scalar_prefetch=2,
            grid=(width // tile,),
            in_specs=[
                pl.BlockSpec((frames, tile), lambda j, off, st: (0, j)),
                pl.BlockSpec((rows, tile), lambda j, off, st: (off[0], st[0] + j)),
            ]
            + specs,
            out_specs=out_specs,
        ),
        input_output_aliases=aliases,
        compiler_params=pltpu.CompilerParams(
            dimension_semantics=("arbitrary",), vmem_limit_bytes=48 * 1024 * 1024
        ),
        cost_estimate=pl.CostEstimate(
            flops=2 * rows * width * frames * 3,
            transcendentals=0,
            bytes_accessed=4 * (rows * width + frames * width + 2 * rows * frames),
        ),
    )(*operands)
    return result if norms else result[0]


def _update_kernel(offset_ref, start_ref, weighted_ref, image_ref, matrix_ref, *rest):
    out_ref = rest[-1]
    frames = image_ref.shape[0]
    weighted_hi, weighted_lo = _split(weighted_ref[...])
    both = jnp.concatenate([weighted_hi, weighted_lo], axis=1)

    def part(index, carry):
        cols = pl.ds(pl.multiple_of(index * SUB, SUB), SUB)
        matrix_hi, matrix_lo = _split(matrix_ref[:, cols])
        paired = lax.dot_general(both, matrix_hi, _TN, preferred_element_type=jnp.float32)
        cross = lax.dot_general(weighted_hi, matrix_lo, _TN, preferred_element_type=jnp.float32)
        out_ref[:, cols] = jnp.maximum(
            image_ref[:, cols] + (paired[:frames] + paired[frames:] + cross), 0.0
        )
        return carry

    lax.fori_loop(0, image_ref.shape[1] // SUB, part, 0)


def update(weighted, image, system, block, rows, first, width, after=None):
    frames = image.shape[0]
    tile = min(TILE, width // 2)
    chunked = image.shape[1] != width
    start = np.array([first // tile], np.int32)
    extra_specs, extra = [], []
    if after is not None:
        block_shape = (8, min(128, after.shape[1]))
        extra_specs, extra = [pl.BlockSpec(block_shape, lambda j, off, st: (0, 0))], [after]
    return pl.pallas_call(
        _update_kernel,
        out_shape=jax.ShapeDtypeStruct((frames, width), jnp.float32),
        grid_spec=pltpu.PrefetchScalarGridSpec(
            num_scalar_prefetch=2,
            grid=(width // tile,),
            in_specs=[
                pl.BlockSpec((rows, frames), lambda j, off, st: (0, 0)),
                pl.BlockSpec((frames, tile), lambda j, off, st: (0, st[0] * chunked + j)),
                pl.BlockSpec((rows, tile), lambda j, off, st: (off[0], st[0] + j)),
            ]
            + extra_specs,
            out_specs=pl.BlockSpec((frames, tile), lambda j, off, st: (0, j)),
        ),
        compiler_params=pltpu.CompilerParams(
            dimension_semantics=("arbitrary",), vmem_limit_bytes=48 * 1024 * 1024
        ),
        cost_estimate=pl.CostEstimate(
            flops=2 * rows * width * frames * 3,
            transcendentals=0,
            bytes_accessed=4 * (rows * width + 2 * frames * width + rows * frames),
        ),
    )(block, start, weighted, image, system, *extra)


def local(system, measured, row_class, band_weight, order):
    cycle_size = lax.axis_size("row")
    position = lax.axis_index("row")
    rows_here = system.shape[0]
    voxels = system.shape[1]
    subblocks = order.shape[1]
    subblock_rows = rows_here // subblocks
    band_hits = (
        row_class[:, None] == jnp.arange(band_weight.shape[0], dtype=jnp.int32)[None, :]
    ).astype(jnp.float32)
    band = jnp.dot(band_hits, band_weight, precision=lax.Precision.HIGHEST)
    sequence = order[0]
    ordered = []
    for which in range(subblocks):
        first_row = sequence[which] * subblock_rows
        ordered.append(
            (
                sequence[which:which + 1],
                lax.dynamic_slice_in_dim(band, first_row, subblock_rows, 0),
                first_row,
            )
        )
    first_rows = lax.dynamic_slice_in_dim(system, ordered[0][2], subblock_rows, 0)
    weight0 = ordered[0][1] / (jnp.sum(first_rows * first_rows, axis=1) + epsilon)
    width = voxels // CHUNKS
    chunks = [jnp.zeros((BATCH_FRAMES, width), jnp.float32) for _ in range(CHUNKS)]
    head = None
    for visit_no in range(STEPS):
        owner = (position - visit_no) % cycle_size
        first_frame = owner * BATCH_FRAMES
        (block0, _, row0), (block1, band1, row1) = ordered
        signal0 = lax.dynamic_slice(measured, (row0, first_frame), (subblock_rows, BATCH_FRAMES))
        signal1 = lax.dynamic_slice(measured, (row1, first_frame), (subblock_rows, BATCH_FRAMES))
        if visit_no == 0:
            residual = signal0
        else:
            total = head
            for index in range(1, CHUNKS):
                total = forward_t(chunks[index], system, block0, subblock_rows, total, index * width)
            residual = signal0 - total
        image = jnp.concatenate(chunks, axis=1)
        image = update(residual * weight0[:, None], image, system, block0, subblock_rows, 0, voxels)
        if visit_no == 0:
            total, norms = forward_t(image, system, block1, subblock_rows, None, 0, True)
            weight1 = band1 / (norms[:, 0] + epsilon)
        else:
            total = forward_t(image, system, block1, subblock_rows, None, 0)
        weighted = (signal1 - total) * weight1[:, None]
        last = visit_no + 1 == STEPS
        steps = 1 if not last else 1 - STEPS
        chunks = []
        for index in range(CHUNKS):
            after = None
            if last and index >= 2:
                after = chunks[index - 2]
            elif not last and index == CHUNKS - 1:
                head = forward_t(chunks[0], system, block0, subblock_rows, None, 0)
                after = head
            piece = update(
                weighted, image, system, block1, subblock_rows, index * width, width, after
            )
            chunks.append(shifted(piece, "row", steps))
    return jnp.concatenate(chunks, axis=1)


def solution(mesh):
    return jax.shard_map(
        local,
        mesh=mesh,
        in_specs=(
            P(("grp", "row"), None),
            P(("grp", "row"), None),
            P(("grp", "row")),
            P("grp"),
            P(("grp", "row"), None),
        ),
        out_specs=P(("grp", "row"), None),
        check_vma=False,
    )
```

```python
import functools

import jax
import numpy as np
import jax.numpy as jnp
from jax import lax
from jax.experimental import pallas as pl
from jax.experimental.pallas import tpu as pltpu
from jax.sharding import PartitionSpec as P

BATCH_FRAMES = 32
STEPS = 6
CHUNKS = 4


epsilon = 1e-06


def shifted(value, axis, steps):
    count = lax.axis_size(axis)
    pairs = [(source, (source + steps) % count) for source in range(count)]
    return lax.ppermute(value, axis, pairs)


TILE = 4096
_DN = (((1,), (1,)), ((), ()))
_TN = (((0,), (0,)), ((), ()))


def _split(value):
    high = value.astype(jnp.bfloat16)
    return high, (value - high.astype(jnp.float32)).astype(jnp.bfloat16)


def _forward_kernel(with_total, with_norms, offset_ref, start_ref, image_ref, matrix_ref, *rest):
    out_ref = rest[1] if with_total else rest[0]
    norm_ref = rest[-1] if with_norms else None

    @pl.when(pl.program_id(0) == 0)
    def _():
        if with_total:
            out_ref[...] = rest[0][...]
        else:
            out_ref[...] = jnp.zeros_like(out_ref)
        if with_norms:
            norm_ref[...] = jnp.zeros_like(norm_ref)

    if with_norms:
        square = matrix_ref[...] * matrix_ref[...]
        norm_ref[...] += jnp.sum(square, axis=1, keepdims=True)

    frames = image_ref.shape[0]
    image_hi, image_lo = _split(image_ref[...])
    both = jnp.concatenate([image_hi, image_lo], axis=0)
    matrix_hi, matrix_lo = _split(matrix_ref[...])
    paired = lax.dot_general(matrix_hi, both, _DN, preferred_element_type=jnp.float32)
    cross = lax.dot_general(matrix_lo, image_hi, _DN, preferred_element_type=jnp.float32)
    out_ref[...] += paired[:, :frames] + paired[:, frames:] + cross


def forward_t(image, system, block, rows, total, first, norms=False):
    frames, width = image.shape
    tile = min(TILE, width // 2)
    start = np.array([first // tile], np.int32)
    operands, specs, aliases = [block, start, image, system], [], {}
    if total is not None:
        operands.append(total)
        specs = [pl.BlockSpec((rows, frames), lambda j, off, st: (0, 0))]
        aliases = {4: 0}
    out_shape = [jax.ShapeDtypeStruct((rows, frames), jnp.float32)]
    out_specs = [pl.BlockSpec((rows, frames), lambda j, off, st: (0, 0))]
    if norms:
        out_shape.append(jax.ShapeDtypeStruct((rows, 1), jnp.float32))
        out_specs.append(pl.BlockSpec((rows, 1), lambda j, off, st: (0, 0)))
    result = pl.pallas_call(
        functools.partial(_forward_kernel, total is not None, norms),
        out_shape=out_shape,
        grid_spec=pltpu.PrefetchScalarGridSpec(
            num_scalar_prefetch=2,
            grid=(width // tile,),
            in_specs=[
                pl.BlockSpec((frames, tile), lambda j, off, st: (0, j)),
                pl.BlockSpec((rows, tile), lambda j, off, st: (off[0], st[0] + j)),
            ]
            + specs,
            out_specs=out_specs,
        ),
        input_output_aliases=aliases,
        compiler_params=pltpu.CompilerParams(
            dimension_semantics=("arbitrary",), vmem_limit_bytes=48 * 1024 * 1024
        ),
        cost_estimate=pl.CostEstimate(
            flops=2 * rows * width * frames * 3,
            transcendentals=0,
            bytes_accessed=4 * (rows * width + frames * width + 2 * rows * frames),
        ),
    )(*operands)
    return result if norms else result[0]


def _update_kernel(offset_ref, start_ref, weighted_ref, image_ref, matrix_ref, *rest):
    out_ref = rest[-1]
    frames = image_ref.shape[0]
    weighted_hi, weighted_lo = _split(weighted_ref[...])
    both = jnp.concatenate([weighted_hi, weighted_lo], axis=1)
    matrix_hi, matrix_lo = _split(matrix_ref[...])
    paired = lax.dot_general(both, matrix_hi, _TN, preferred_element_type=jnp.float32)
    cross = lax.dot_general(weighted_hi, matrix_lo, _TN, preferred_element_type=jnp.float32)
    out_ref[...] = jnp.maximum(
        image_ref[...] + (paired[:frames] + paired[frames:] + cross), 0.0
    )


def update(weighted, image, system, block, rows, first, width, after=None):
    frames = image.shape[0]
    tile = min(TILE, width // 2)
    chunked = image.shape[1] != width
    start = np.array([first // tile], np.int32)
    extra_specs, extra = [], []
    if after is not None:
        block_shape = (8, min(128, after.shape[1]))
        extra_specs, extra = [pl.BlockSpec(block_shape, lambda j, off, st: (0, 0))], [after]
    return pl.pallas_call(
        _update_kernel,
        out_shape=jax.ShapeDtypeStruct((frames, width), jnp.float32),
        grid_spec=pltpu.PrefetchScalarGridSpec(
            num_scalar_prefetch=2,
            grid=(width // tile,),
            in_specs=[
                pl.BlockSpec((rows, frames), lambda j, off, st: (0, 0)),
                pl.BlockSpec((frames, tile), lambda j, off, st: (0, st[0] * chunked + j)),
                pl.BlockSpec((rows, tile), lambda j, off, st: (off[0], st[0] + j)),
            ]
            + extra_specs,
            out_specs=pl.BlockSpec((frames, tile), lambda j, off, st: (0, j)),
        ),
        compiler_params=pltpu.CompilerParams(
            dimension_semantics=("arbitrary",), vmem_limit_bytes=48 * 1024 * 1024
        ),
        cost_estimate=pl.CostEstimate(
            flops=2 * rows * width * frames * 3,
            transcendentals=0,
            bytes_accessed=4 * (rows * width + 2 * frames * width + rows * frames),
        ),
    )(block, start, weighted, image, system, *extra)


def local(system, measured, row_class, band_weight, order):
    cycle_size = lax.axis_size("row")
    position = lax.axis_index("row")
    rows_here = system.shape[0]
    voxels = system.shape[1]
    subblocks = order.shape[1]
    subblock_rows = rows_here // subblocks
    band_hits = (
        row_class[:, None] == jnp.arange(band_weight.shape[0], dtype=jnp.int32)[None, :]
    ).astype(jnp.float32)
    band = jnp.dot(band_hits, band_weight, precision=lax.Precision.HIGHEST)
    sequence = order[0]
    ordered = []
    for which in range(subblocks):
        first_row = sequence[which] * subblock_rows
        ordered.append(
            (
                sequence[which:which + 1],
                lax.dynamic_slice_in_dim(band, first_row, subblock_rows, 0),
                first_row,
            )
        )
    first_rows = lax.dynamic_slice_in_dim(system, ordered[0][2], subblock_rows, 0)
    weight0 = ordered[0][1] / (jnp.sum(first_rows * first_rows, axis=1) + epsilon)
    width = voxels // CHUNKS
    chunks = [jnp.zeros((BATCH_FRAMES, width), jnp.float32) for _ in range(CHUNKS)]
    head = None
    for visit_no in range(STEPS):
        owner = (position - visit_no) % cycle_size
        first_frame = owner * BATCH_FRAMES
        (block0, _, row0), (block1, band1, row1) = ordered
        signal0 = lax.dynamic_slice(measured, (row0, first_frame), (subblock_rows, BATCH_FRAMES))
        signal1 = lax.dynamic_slice(measured, (row1, first_frame), (subblock_rows, BATCH_FRAMES))
        if visit_no == 0:
            residual = signal0
        else:
            total = head
            for index in range(1, CHUNKS):
                total = forward_t(chunks[index], system, block0, subblock_rows, total, index * width)
            residual = signal0 - total
        image = jnp.concatenate(chunks, axis=1)
        image = update(residual * weight0[:, None], image, system, block0, subblock_rows, 0, voxels)
        if visit_no == 0:
            total, norms = forward_t(image, system, block1, subblock_rows, None, 0, True)
            weight1 = band1 / (norms[:, 0] + epsilon)
        else:
            total = forward_t(image, system, block1, subblock_rows, None, 0)
        weighted = (signal1 - total) * weight1[:, None]
        last = visit_no + 1 == STEPS
        steps = 1 if not last else 1 - STEPS
        chunks = []
        for index in range(CHUNKS):
            after = None
            if last and index >= 2:
                after = chunks[0]
            elif not last and index == CHUNKS - 1:
                head = forward_t(chunks[0], system, block0, subblock_rows, None, 0)
                after = head
            piece = update(
                weighted, image, system, block1, subblock_rows, index * width, width, after
            )
            chunks.append(shifted(piece, "row", steps))
    return jnp.concatenate(chunks, axis=1)


def solution(mesh):
    return jax.shard_map(
        local,
        mesh=mesh,
        in_specs=(
            P(("grp", "row"), None),
            P(("grp", "row"), None),
            P(("grp", "row")),
            P("grp"),
            P(("grp", "row"), None),
        ),
        out_specs=P(("grp", "row"), None),
        check_vma=False,
    )
```
